32 devices in a mesh: row: 8 (over y, x, core), col: 4 (over z).
Axes of the slice: x: 2, y: 2, z: 4, core: 2. Of those that a mesh axis runs over, the one named last changes fastest.
Arguments:
- relu21_preact: bfloat16 [256, 256, 128], P('row', 'col'), may hold values from -6 to 6
- relu22_preact: bfloat16 [256, 256, 128], P('row', 'col'), may hold values from -600 to 600
- relu31_preact: bfloat16 [128, 128, 256], P('row', 'col'), may hold values from -6 to 6
- relu32_preact: bfloat16 [128, 128, 256], P('row', 'col'), may hold values from -6 to 6
- relu33_preact: bfloat16 [128, 128, 256], P('row', 'col'), may hold values from -600 to 600
- target22_preact: bfloat16 [256, 256, 128], P('row', 'col'), may hold values from -600 to 600
- target33_preact: bfloat16 [128, 128, 256], P('row', 'col'), may hold values from -600 to 600
- pool1_argmax: int32 [256, 16384], P('row', 'col'), may hold values from 0 to 3
- pool2_argmax: int32 [128, 16384], P('row', 'col'), may hold values from 0 to 3
- linear2_weight: float32 [128], replicated, may hold values from 0.2 to 2
- linear3_weight: float32 [256], replicated, may hold values from 0.2 to 2
- kernel21: bfloat16 [128, 576], replicated, may hold values from -0.25 to 0.25
- kernel22: bfloat16 [128, 1152], replicated, may hold values from -0.1875 to 0.1875
- kernel31: bfloat16 [256, 1152], replicated, may hold values from -0.1875 to 0.1875
- kernel32: bfloat16 [256, 2304], replicated, may hold values from -0.125 to 0.125
- kernel33: bfloat16 [256, 2304], replicated, may hold values from -0.125 to 0.125
Outputs:
- relu12_gradient: bfloat16 [512, 32768], P('row', 'col')
The draws below stay inside these ranges and needn't reach their ends.
Inputs may be any that keep to these rules, and one draw needn't show every extreme that they name: `pool1_argmax`: the position of the maximum in each 2x2 window, 0 top left, 1 top right, 2 bottom left, 3 bottom right; entry [r, c * 64 + ch] belongs to pooled cell (r, c) and channel ch. `pool2_argmax`: as for pool1_argmax, with 128 channels.
All inputs are finite; a program needn't handle non-finite values.
Results may differ from the reference program's by a relative error of at most 0.0059.
Values may be sent and summed in bfloat16 or wider, within the bound.
A program may use at most 64 MiB of HBM per device.

```python
import math
import jax
import jax.numpy as jnp
from jax import lax

CH1 = 64
CH2 = 128
CH3 = 256
HEIGHT = 128
WIDTH = 128


def tap_values(key, salt, height, breadth, channels):
    folded = jax.random.fold_in(key, salt)
    streams = jax.random.split(folded, 3)
    spread = math.log(10.0)
    values = jnp.clip(jax.random.normal(streams[2], (height, breadth, channels), jnp.float32), -4.0, 4.0)
    channel_scale = jnp.exp(jax.random.uniform(streams[0], (channels,), jnp.float32, 0.0, spread))
    pixel_scale = jnp.exp(jax.random.uniform(streams[1], (height, breadth, 1), jnp.float32, 0.0, spread))
    return (values * channel_scale * pixel_scale).astype(jnp.bfloat16)


def draw_relu22_preact(key, part):
    return tap_values(key, 11, 2 * HEIGHT, 2 * WIDTH, CH2)


def draw_relu33_preact(key, part):
    return tap_values(key, 12, HEIGHT, WIDTH, CH3)


def draw_target22_preact(key, part):
    return tap_values(key, 13, 2 * HEIGHT, 2 * WIDTH, CH2)


def draw_target33_preact(key, part):
    return tap_values(key, 14, HEIGHT, WIDTH, CH3)


def plant(drawn, own_key, least, top_value):
    index_at = [jax.random.randint(jax.random.fold_in(own_key, axis), (), 0, length) for axis, length in enumerate(drawn.shape)]
    longest = drawn.shape.index(max(drawn.shape))
    next_to = index_at[:longest] + [(index_at[longest] + 1) % drawn.shape[longest]] + index_at[longest + 1:]
    return drawn.at[tuple(index_at)].set(least).at[tuple(next_to)].set(top_value)


def levels(stream_key, dims, cuts, smallest, high):
    def one(dim, shards_of):
        draws = jax.random.uniform(jax.random.fold_in(jax.random.fold_in(stream_key, 6), dim), (shards_of,), jnp.float32, smallest / len(cuts), high / len(cuts))
        return jnp.repeat(jnp.exp(draws), dims[dim] // shards_of).reshape((-1,) + (1,) * (len(dims) - dim - 1))

    gain = one(*cuts[0])
    for cut in cuts[1:]:
        gain = gain * one(*cut)
    return gain


def centred(rng, shape, scale, limit, cuts=(), held_as=jnp.bfloat16):
    entries = scale * jax.random.normal(rng, shape, jnp.float32)
    if cuts:
        entries = entries * levels(rng, shape, cuts, -0.22, 0.18)
    return jnp.clip(entries, -limit, limit).astype(held_as)


def setup_inputs(seed: int = 0) -> dict:
    splits = jax.random.split(jax.random.key(seed), 17)
    return {
        "relu21_preact": centred(splits[0], (2 * HEIGHT, 2 * WIDTH, CH2), 1.0, 6.0, ((0, 8), (1, 4))),
        "relu22_preact": draw_relu22_preact(jax.random.fold_in(splits[16], 71), 0),
        "relu31_preact": centred(splits[2], (HEIGHT, WIDTH, CH3), 1.0, 6.0, ((0, 8), (1, 4))),
        "relu32_preact": centred(splits[3], (HEIGHT, WIDTH, CH3), 1.0, 6.0, ((0, 8), (1, 4))),
        "relu33_preact": draw_relu33_preact(jax.random.fold_in(splits[16], 71), 0),
        "target22_preact": draw_target22_preact(jax.random.fold_in(splits[16], 71), 0),
        "target33_preact": draw_target33_preact(jax.random.fold_in(splits[16], 71), 0),
        "pool1_argmax": plant(jax.random.randint(splits[7], (2 * HEIGHT, 2 * WIDTH * CH1), 0, 4), jax.random.fold_in(splits[7], 1), 0, 3).astype(jnp.int32),
        "pool2_argmax": plant(jax.random.randint(splits[8], (HEIGHT, WIDTH * CH2), 0, 4), jax.random.fold_in(splits[8], 1), 0, 3).astype(jnp.int32),
        "linear2_weight": jnp.clip(jnp.exp(jax.random.uniform(splits[9], (CH2,), jnp.float32, math.log(0.2), math.log(2.0))), 0.2, 2.0),
        "linear3_weight": jnp.clip(jnp.exp(jax.random.uniform(splits[10], (CH3,), jnp.float32, math.log(0.2), math.log(2.0))), 0.2, 2.0),
        "kernel21": centred(splits[11], (CH2, 9 * CH1), (9 * CH1) ** -0.5, 0.25),
        "kernel22": centred(splits[12], (CH2, 9 * CH2), (9 * CH2) ** -0.5, 0.1875),
        "kernel31": centred(splits[13], (CH3, 9 * CH2), (9 * CH2) ** -0.5, 0.1875),
        "kernel32": centred(splits[14], (CH3, 9 * CH3), (9 * CH3) ** -0.5, 0.125),
        "kernel33": centred(splits[15], (CH3, 9 * CH3), (9 * CH3) ** -0.5, 0.125),
    }


EPSILON = 1e-06

def inject(preact, target, weight):
    feature = jnp.maximum(preact.astype(jnp.float32), 0.0)
    wanted = jnp.maximum(target.astype(jnp.float32), 0.0)
    feature_norm = jnp.sqrt(lax.optimization_barrier(jnp.mean(feature * feature, axis=-1, keepdims=True)) + EPSILON)
    wanted_norm = jnp.sqrt(lax.optimization_barrier(jnp.mean(wanted * wanted, axis=-1, keepdims=True)) + EPSILON)
    scaled = feature / feature_norm
    excess = 2.0 * weight * (scaled - wanted / wanted_norm)
    return (excess - scaled * lax.optimization_barrier(jnp.mean(excess * scaled, axis=-1, keepdims=True))) / feature_norm

def masked(preact, values):
    return jnp.where(preact > 0, values, 0.0).astype(jnp.bfloat16)

def unpool(values, argmax_rows):
    height, breadth, channels = values.shape
    position = argmax_rows.reshape(height, breadth, channels)
    stripes = []
    for vertical in range(2):
        halves = [jnp.where(position == 2 * vertical + lateral, values, 0.0) for lateral in range(2)]
        stripes.append(jnp.stack(halves, axis=2))
    return jnp.stack(stripes, axis=1).reshape(2 * height, 2 * breadth, channels)

def back_conv(gradient, kernel):
    outputs = kernel.shape[0]
    channels_in = kernel.shape[1] // 9
    flipped = kernel.reshape(outputs, 3, 3, channels_in)[:, ::-1, ::-1, :]
    flipped = flipped.transpose(1, 2, 0, 3).astype(jnp.float32)
    result = lax.conv_general_dilated(gradient.astype(jnp.float32)[None], flipped, (1, 1), 'SAME', dimension_numbers=('NHWC', 'HWIO', 'NHWC'), precision=lax.Precision.HIGHEST)
    return result[0]

def reference(relu21_preact, relu22_preact, relu31_preact, relu32_preact, relu33_preact, target22_preact, target33_preact, pool1_argmax, pool2_argmax, linear2_weight, linear3_weight, kernel21, kernel22, kernel31, kernel32, kernel33):
    seeded = masked(relu33_preact, inject(relu33_preact, target33_preact, linear3_weight))
    gradient32 = masked(relu32_preact, back_conv(seeded, kernel33))
    gradient31 = masked(relu31_preact, back_conv(gradient32, kernel32))
    pooled2 = back_conv(gradient31, kernel31)
    arriving = unpool(pooled2, pool2_argmax) + inject(relu22_preact, target22_preact, linear2_weight)
    gradient22 = masked(relu22_preact, arriving)
    gradient21 = masked(relu21_preact, back_conv(gradient22, kernel22))
    pooled1 = back_conv(gradient21, kernel21)
    result = unpool(pooled1, pool1_argmax).astype(jnp.bfloat16)
    return result.reshape(result.shape[0], -1)
```

```python
import functools

import jax
import jax.numpy as jnp
from jax import lax
from jax.experimental import pallas as pl
from jax.experimental.pallas import tpu as pltpu
from jax.sharding import PartitionSpec as P

EPSILON = 1e-06
MESH = pl.DeviceIdType.MESH
F32 = jnp.float32
BF16 = jnp.bfloat16
SIDE = 8
OFF3 = 6
OFF2 = 4
OFFU = 2
DIRS = ((-1, 0), (1, 0), (0, -1), (0, 1), (-1, -1), (-1, 1), (1, -1), (1, 1))
HALOS = (4, 4, 3, 2, 2, 2, 1)


def message_shape(shape, halo, d):
    dr, dc = d
    return (halo if dr else shape[0], SIDE if dc else shape[1], shape[2])


def source_slices(shape, halo, d):
    dr, dc = d
    rows = slice(0, shape[0]) if dr == 0 else (slice(0, halo) if dr < 0 else slice(shape[0] - halo, shape[0]))
    cols = slice(0, shape[1]) if dc == 0 else (slice(0, SIDE) if dc < 0 else slice(shape[1] - SIDE, shape[1]))
    return rows, cols


def landing_slices(shape, halo, off, d):
    dr, dc = d
    first, count = {0: (0, shape[0]), -1: (shape[0], halo), 1: (-halo, halo)}[dr]
    if dc == 0:
        cols = slice(0, shape[1])
    elif dc < 0:
        cols = slice(shape[1], shape[1] + SIDE)
    else:
        cols = slice(shape[1] + SIDE, shape[1] + 2 * SIDE)
        first -= 1
    return slice(off + first, off + first + count), cols


def place(axes):
    return tuple(lax.axis_index(a) for a in axes)


def reachable(axes, counts, d, sign):
    checks = []
    for axis, count, step in zip(axes, counts, d):
        if step:
            target = lax.axis_index(axis) + sign * step
            checks.append(target >= 0 if sign * step < 0 else target < count)
    ok = checks[0]
    for c in checks[1:]:
        ok = jnp.logical_and(ok, c)
    return ok


def exchange_kernel(axes, counts, shapes, *refs):
    n = len(shapes)
    inputs, pool = refs[:n], refs[n]
    outs = refs[n + 1 : n + 1 + 8 * n]
    pool_outs = refs[n + 1 + 8 * n : n + 1 + 8 * n + 8]
    edge, edge_rows, local_sem, send_sem, recv_sem = refs[n + 1 + 8 * n + 8 :]
    depth = pool.shape[0]
    width = pool.shape[1] // 128
    top = pltpu.make_async_copy(pool.at[pl.ds(0, 8)], edge.at[0], local_sem.at[0])
    low = pltpu.make_async_copy(pool.at[pl.ds(depth - 8, 8)], edge.at[1], local_sem.at[1])
    top.start()
    low.start()
    barrier = pltpu.get_barrier_semaphore()
    me = place(axes)
    for d in DIRS:
        @pl.when(reachable(axes, counts, d, 1))
        def _():
            pl.semaphore_signal(barrier, inc=1, device_id=(me[0] + d[0], me[1] + d[1]), device_id_type=MESH)
    spans = [1 + jnp.minimum(m, 1) + jnp.minimum(c - 1 - m, 1) for m, c in zip(me, counts)]
    pl.semaphore_wait(barrier, spans[0] * spans[1] - 1)

    def copy(a, k):
        d = DIRS[k]
        if a < n:
            rows, cols = source_slices(shapes[a], HALOS[a], d)
            src, dst = inputs[a].at[rows, cols], outs[8 * a + k]
        else:
            dst = pool_outs[k]
            if d[1] == 0:
                src = edge_rows.at[0 if d[0] < 0 else 1]
            else:
                rows = {0: slice(0, depth), -1: slice(0, 8), 1: slice(depth - 8, depth)}[d[0]]
                lanes = slice(0, 128) if d[1] < 0 else slice((width - 1) * 128, width * 128)
                src = pool.at[rows, lanes]
        return pltpu.make_async_remote_copy(
            src_ref=src, dst_ref=dst, send_sem=send_sem.at[a, k], recv_sem=recv_sem.at[a, k],
            device_id=(me[0] + d[0], me[1] + d[1]), device_id_type=MESH)

    for a in range(n):
        for k in range(8):
            @pl.when(reachable(axes, counts, DIRS[k], 1))
            def _():
                copy(a, k).start()
    top.wait()
    low.wait()
    for j in range(width):
        edge_rows[0, j : j + 1, :] = edge[0, 0:1, j * 128 : (j + 1) * 128]
        edge_rows[1, j : j + 1, :] = edge[1, 7:8, j * 128 : (j + 1) * 128]
    for k in range(8):
        @pl.when(reachable(axes, counts, DIRS[k], 1))
        def _():
            copy(n, k).start()
    for a in range(n + 1):
        for k in range(8):
            @pl.when(reachable(axes, counts, DIRS[k], 1))
            def _():
                copy(a, k).wait_send()

            @pl.when(reachable(axes, counts, DIRS[k], -1))
            def _():
                copy(a, k).wait_recv()


def injected(p, t, weight):
    f = jnp.maximum(p, 0.0)
    g = jnp.maximum(t, 0.0)
    rinv = lax.rsqrt(jnp.mean(f * f, axis=-1, keepdims=True) + EPSILON)
    sinv = lax.rsqrt(jnp.mean(g * g, axis=-1, keepdims=True) + EPSILON)
    u = f * rinv
    e = weight * (u - g * sinv)
    return (e - u * jnp.mean(e * u, axis=-1, keepdims=True)) * rinv


def shifted_sum(z, n):
    length = z.shape[0]
    return pltpu.roll(z[:, :n], length - 1, 0) + z[:, n : 2 * n] + pltpu.roll(z[:, 2 * n :], 1, 0)


def conv_rows(x, w, first, rows, stride, n):
    length = rows * stride + 32
    start = first * stride - 16
    parts = [x[pl.ds(pl.multiple_of(start + (1 - dy) * stride, 16), length), :] for dy in range(3)]
    z = jnp.dot(jnp.concatenate(parts, axis=1), w[...], preferred_element_type=F32)
    return shifted_sum(z, n)[16 : 16 + rows * stride]


def body_kernel(axes, counts, shapes, *refs):
    n = len(shapes)
    inputs = refs[:n]
    pool1, pool2, lin2, lin3, k21, k22, k31, k32, k33 = refs[n : n + 9]
    halos = refs[n + 9 : n + 9 + 8 * n]
    pool_halos = refs[n + 9 + 8 * n : n + 17 + 8 * n]
    out = refs[n + 17 + 8 * n]
    scratch = refs[n + 18 + 8 * n :]
    bufs = scratch[:n]
    (x33, x32, x31, x22, x21, w33, w32, w31, w22, w21, k21v, p1, p2, prow, pcol, pcor, upy, upp, yt, tmp, res,
     in_sem, halo_sem, w_sem, pool_sem, ph_sem, out_sem) = scratch[n:]
    off = [OFF3, OFF3, OFF3, OFF3, OFF2, OFF2, OFF2]
    h3, wd3 = shapes[0][0], shapes[0][1]
    h2, wd2 = shapes[4][0], shapes[4][1]
    s3, s2 = wd3 + 2 * SIDE, wd2 + 2 * SIDE

    def own(a):
        return pltpu.make_async_copy(
            inputs[a], bufs[a].at[off[a] : off[a] + shapes[a][0], 0 : shapes[a][1]], in_sem.at[a])

    def halo(a, k):
        rows, cols = landing_slices(shapes[a], HALOS[a], off[a], DIRS[k])
        return pltpu.make_async_copy(halos[8 * a + k], bufs[a].at[rows, cols], halo_sem.at[a, k])

    def weights(i):
        k, w = ((k33, w33), (k32, w32), (k31, w31), (k22, w22))[i]
        o, cols = k.shape[0], k.shape[1] // 3
        return [pltpu.make_async_copy(k.at[:, dy * cols : (dy + 1) * cols], w.at[dy * o : (dy + 1) * o], w_sem.at[i, dy])
                for dy in range(3)]

    def pool_halo(k):
        dr, dc = DIRS[k]
        dst = prow.at[k] if dc == 0 else (pcol.at[k - 2] if dr == 0 else pcor.at[k - 4])
        return pltpu.make_async_copy(pool_halos[k], dst, ph_sem.at[k])

    others = (pltpu.make_async_copy(k21, k21v, pool_sem.at[0]), pltpu.make_async_copy(pool1, p1, pool_sem.at[1]),
              pltpu.make_async_copy(pool2, p2, pool_sem.at[2]))

    def arrive(a, act):
        act(own(a))
        for k in range(8):
            @pl.when(reachable(axes, counts, DIRS[k], -1))
            def _():
                act(halo(a, k))

    start, wait = (lambda c: c.start()), (lambda c: c.wait())
    arrive(0, start)
    arrive(1, start)
    for c in weights(0):
        c.start()
    arrive(2, start)
    for c in weights(1):
        c.start()
    arrive(3, start)
    for c in weights(2):
        c.start()
    for c in others:
        c.start()
    for k in range(8):
        pool_halo(k).start()
    for a in (4, 5, 6):
        arrive(a, start)
    for c in weights(3):
        c.start()
    for a in (0, 2, 3, 4, 6):
        for k in range(8):
            @pl.when(jnp.logical_not(reachable(axes, counts, DIRS[k], -1)))
            def _():
                rows, cols = landing_slices(shapes[a], HALOS[a], off[a], DIRS[k])
                dst = bufs[a].at[rows, cols]
                dst[...] = jnp.zeros(dst.shape, BF16)

    arrive(0, wait)
    arrive(1, wait)
    c3 = shapes[0][2]
    c2 = shapes[4][2]
    weight3 = 2.0 * lin3[...]
    weight2 = 2.0 * lin2[...]

    @pl.loop(0, bufs[0].shape[0] // 2)
    def _(i):
        p = bufs[0][pl.ds(2 * i, 2)].reshape(2 * s3, c3).astype(F32)
        t = bufs[1][pl.ds(2 * i, 2)].reshape(2 * s3, c3).astype(F32)
        seed = jnp.where(p > 0, injected(p, t, weight3), 0.0).astype(BF16)
        x33[pl.ds(pl.multiple_of(2 * i * s3, 16), 2 * s3), :] = seed

    def masked_conv(x, w, p, y, first, rows, steps, stride, channels):
        @pl.loop(0, steps)
        def _(i):
            at = first + i * rows
            o = conv_rows(x, w, at, rows, stride, channels)
            pre = p[pl.ds(at, rows)].reshape(rows * stride, channels).astype(F32)
            y[pl.ds(pl.multiple_of(at * stride, 16), rows * stride), :] = jnp.where(pre > 0, o, 0.0).astype(BF16)

    arrive(2, wait)
    for c in weights(0):
        c.wait()
    masked_conv(x33, w33, bufs[2], x32, OFF3 - 4, (h3 + 8) // 3, 3, s3, c3)
    arrive(3, wait)
    for c in weights(1):
        c.wait()
    masked_conv(x32, w32, bufs[3], x31, OFF3 - 3, (h3 + 5) // 3, 3, s3, c3)

    for c in others:
        c.wait()
    for k in range(8):
        pool_halo(k).wait()
    for j in range(wd3):
        for i0 in range(0, h3, 8):
            blk = p2[i0 : i0 + 8, j * 128 : (j + 1) * 128]
            for b in range(2):
                upp[pl.ds((OFFU + i0) * s2 + 2 * j + b, 8, stride=s2), :] = blk
    for b in range(2):
        upp[pl.ds((OFFU + h3) * s2 + b, wd3, stride=2), :] = prow[0]
        upp[pl.ds((OFFU - 1) * s2 + b, wd3, stride=2), :] = prow[1]
        for i0 in range(0, h3, 8):
            upp[pl.ds((OFFU + i0) * s2 + wd2 + b, 8, stride=s2), :] = pcol[0, i0 : i0 + 8]
            upp[pl.ds((OFFU + i0) * s2 + s2 - 2 + b, 8, stride=s2), :] = pcol[1, i0 : i0 + 8]
        upp[(OFFU + h3) * s2 + wd2 + b : (OFFU + h3) * s2 + wd2 + b + 1, :] = pcor[0, 0:1]
        upp[(OFFU + h3) * s2 + s2 - 2 + b : (OFFU + h3) * s2 + s2 - 2 + b + 1, :] = pcor[1, 0:1]
        upp[(OFFU - 1) * s2 + wd2 + b : (OFFU - 1) * s2 + wd2 + b + 1, :] = pcor[2, 7:8]
        upp[(OFFU - 1) * s2 + s2 - 2 + b : (OFFU - 1) * s2 + s2 - 2 + b + 1, :] = pcor[3, 7:8]

    for c in weights(2):
        c.wait()
    rows31 = (h3 + 4) // 4

    @pl.loop(0, 4)
    def _(i):
        o = conv_rows(x31, w31, OFF3 - 2 + i * rows31, rows31, s3, c2)
        for q in range(rows31):
            row = i * rows31 + q
            base = row * s2
            y = o[q * s3 : (q + 1) * s3]
            for b in range(2):
                upy[pl.ds(base + b, wd3, stride=2), :] = y[:wd3]
                upy[pl.ds(base + wd2 + b, 4, stride=2), :] = y[wd3 : wd3 + 4]
                upy[pl.ds(base + s2 + s2 - 8 + b, 4, stride=2), :] = y[s3 - 4 :]

    arrive(4, wait)
    arrive(5, wait)
    main = s2 - 8
    par = lax.broadcasted_iota(jnp.int32, (s2, 128), 0) % 2

    @pl.loop(0, h2 + 5)
    def _(i):
        for_row = i + OFF2 - 3
        r0 = (i + 1) // 2 + OFFU - 2
        a0 = (i + 1) % 2
        r1 = (i + 2) // 2 + OFFU - 2
        a1 = (i + 2) % 2
        at0 = pl.multiple_of(r0 * s2, 8)
        at1 = pl.multiple_of(r1 * s2 + main, 8)
        y = jnp.concatenate([upy[pl.ds(at0, main), :], upy[pl.ds(at1, 8), :]], axis=0)
        m = jnp.concatenate([upp[pl.ds(at0, main), :] - 2 * a0, upp[pl.ds(at1, 8), :] - 2 * a1], axis=0)
        p = bufs[4][for_row].astype(F32)
        t = bufs[5][for_row].astype(F32)
        arriving = jnp.where(m == par, y, 0.0) + injected(p, t, weight2)
        x22[pl.ds(pl.multiple_of(for_row * s2, 16), s2), :] = jnp.where(p > 0, arriving, 0.0).astype(BF16)

    arrive(6, wait)
    for c in weights(3):
        c.wait()
    masked_conv(x22, w22, bufs[6], x21, OFF2 - 2, (h2 + 3) // 5, 5, s2, c2)

    low_half = lax.broadcasted_iota(jnp.int32, (c2, 128), 1) < 64
    for tap in range(9):
        dy, dx = tap // 3, tap % 3
        width = min(128, 576 - (tap // 2) * 128)
        blk = k21v[:, (tap // 2) * 128 : (tap // 2) * 128 + width].astype(F32)
        if width < 128:
            blk = jnp.concatenate([blk, blk], axis=1)
        else:
            turned = pltpu.roll(blk, 64, 1)
            blk = jnp.where(low_half, blk, turned) if tap % 2 == 0 else jnp.where(low_half, turned, blk)
        w21[dy * c2 : (dy + 1) * c2, dx * 128 : (dx + 1) * 128] = blk.astype(BF16)

    rows21 = 8

    @pl.loop(0, h2 // rows21)
    def _(i):
        o = conv_rows(x21, w21, OFF2 + i * rows21, rows21, s2, 128)
        for q in range(rows21):
            for j0 in range(0, wd2, 8):
                y = o[q * s2 + j0 : q * s2 + j0 + 8]
                for a in range(2):
                    yt[pl.ds(j0 * 2 * h2 + 2 * (i * rows21 + q) + a, 8, stride=2 * h2), :] = y

    lane_low = lax.broadcasted_iota(jnp.int32, (2 * h2, 128), 1) < 64
    want = (lax.broadcasted_iota(jnp.int32, (2 * h2, 128), 0) % 2) * 2 + jnp.where(lane_low, 0, 1)

    @pl.loop(0, wd2 // 2)
    def _(g):
        lanes = pl.ds(pl.multiple_of(g * 128, 128), 128)
        blk = p1[:, lanes]
        for a in range(2):
            tmp[pl.ds(a, h2, stride=2), :] = blk
        m = tmp[...]
        turned = pltpu.roll(m, 64, 1)
        for e in range(2):
            y = yt[pl.ds(pl.multiple_of((2 * g + e) * 2 * h2, 8), 2 * h2), :]
            sel = jnp.where(lane_low, m, turned) if e == 0 else jnp.where(lane_low, turned, m)
            res[:, pl.ds(pl.multiple_of((2 * g + e) * 128, 128), 128)] = jnp.where(sel == want, y, 0.0).astype(BF16)

    done = pltpu.make_async_copy(res, out, out_sem)
    done.start()
    done.wait()


def shards(axes, counts, relu21, relu22, relu31, relu32, relu33, target22, target33, pool1, pool2, lin2, lin3,
           k21, k22, k31, k32, k33):
    tensors = (relu33, target33, relu32, relu31, relu22, target22, relu21)
    shapes = tuple(t.shape for t in tensors)
    n = len(tensors)
    h3, wd3, c3 = relu33.shape
    h2, wd2, c2 = relu22.shape
    s3, s2 = wd3 + 2 * SIDE, wd2 + 2 * SIDE
    anywhere = pl.BlockSpec(memory_space=pl.ANY)
    vmem = pl.BlockSpec(memory_space=pltpu.VMEM)
    halo_shapes = [jax.ShapeDtypeStruct(message_shape(s, h, d), BF16) for s, h in zip(shapes, HALOS) for d in DIRS]
    for d in DIRS:
        shape = (wd3, 128) if d[1] == 0 else ((h3, 128) if d[0] == 0 else (8, 128))
        halo_shapes.append(jax.ShapeDtypeStruct(shape, jnp.int32))
    halos = pl.pallas_call(
        functools.partial(exchange_kernel, axes, counts, shapes),
        out_shape=halo_shapes,
        in_specs=[anywhere] * (n + 1),
        out_specs=[anywhere] * len(halo_shapes),
        scratch_shapes=[
            pltpu.VMEM((2, 8, pool2.shape[1]), jnp.int32),
            pltpu.VMEM((2, wd3, 128), jnp.int32),
            pltpu.SemaphoreType.DMA((2,)),
            pltpu.SemaphoreType.DMA((n + 1, 8)),
            pltpu.SemaphoreType.DMA((n + 1, 8)),
        ],
        compiler_params=pltpu.CompilerParams(collective_id=0, has_side_effects=True),
        name="exchange",
    )(*tensors, pool2)
    rows3, rows2 = h3 + 2 * OFF3, h2 + 2 * OFF2
    scratch = [pltpu.VMEM((rows3, s3, c3), BF16)] * 4 + [pltpu.VMEM((rows2, s2, c2), BF16)] * 3
    scratch += [pltpu.VMEM((rows3 * s3, c3), BF16)] * 3 + [pltpu.VMEM((rows2 * s2, c2), BF16)] * 2
    scratch += [pltpu.VMEM((3 * k.shape[0], k.shape[1] // 3), BF16) for k in (k33, k32, k31, k22)]
    scratch += [
        pltpu.VMEM((3 * c2, 384), BF16),
        pltpu.VMEM(k21.shape, BF16),
        pltpu.VMEM(pool1.shape, jnp.int32),
        pltpu.VMEM(pool2.shape, jnp.int32),
        pltpu.VMEM((2, wd3, 128), jnp.int32),
        pltpu.VMEM((2, h3, 128), jnp.int32),
        pltpu.VMEM((4, 8, 128), jnp.int32),
        pltpu.VMEM(((h3 + 2 * OFFU + 1) * s2, 128), F32),
        pltpu.VMEM(((h3 + 2 * OFFU + 1) * s2, 128), jnp.int32),
        pltpu.VMEM((wd2 * 2 * h2, 128), F32),
        pltpu.VMEM((2 * h2, 128), jnp.int32),
        pltpu.VMEM((2 * h2, wd2 * 128), BF16),
        pltpu.SemaphoreType.DMA((n,)),
        pltpu.SemaphoreType.DMA((n, 8)),
        pltpu.SemaphoreType.DMA((4, 3)),
        pltpu.SemaphoreType.DMA((3,)),
        pltpu.SemaphoreType.DMA((8,)),
        pltpu.SemaphoreType.DMA(()),
    ]
    return pl.pallas_call(
        functools.partial(body_kernel, axes, counts, shapes),
        out_shape=jax.ShapeDtypeStruct((2 * h2, wd2 * 128), BF16),
        in_specs=[anywhere] * (n + 2) + [vmem] * 2 + [anywhere] * (5 + len(halo_shapes)),
        out_specs=anywhere,
        scratch_shapes=scratch,
        compiler_params=pltpu.CompilerParams(vmem_limit_bytes=56 * 1024 * 1024),
        name="body",
    )(*tensors, pool1, pool2, lin2.reshape(1, c2), lin3.reshape(1, c3), k21, k22, k31, k32, k33, *halos)


def solution(mesh):
    axes = ("row", "col")
    counts = tuple(mesh.shape[a] for a in axes)
    cells = P("row", "col", None)
    in_specs = (cells,) * 7 + (P("row", "col"),) * 2 + (P(),) * 7
    return jax.shard_map(functools.partial(shards, axes, counts), mesh=mesh, in_specs=in_specs,
                         out_specs=P("row", "col"), check_vma=False)
```

```python
import functools

import jax
import jax.numpy as jnp
from jax import lax
from jax.experimental import pallas as pl
from jax.experimental.pallas import tpu as pltpu
from jax.sharding import PartitionSpec as P

EPSILON = 1e-06
MESH = pl.DeviceIdType.MESH
F32 = jnp.float32
BF16 = jnp.bfloat16
SIDE = 8
OFF3 = 6
OFF2 = 4
OFFU = 2
DIRS = ((-1, 0), (1, 0), (0, -1), (0, 1), (-1, -1), (-1, 1), (1, -1), (1, 1))


WIDTHS = (4, 4, 2, 2, 2, 1)
ROWS = (4, 3, 2, 2, 2, 1)


def reachable(axes, counts, d, sign):
    checks = []
    for axis, count, step in zip(axes, counts, d):
        if step:
            target = lax.axis_index(axis) + sign * step
            checks.append(target >= 0 if sign * step < 0 else target < count)
    ok = checks[0]
    for c in checks[1:]:
        ok = jnp.logical_and(ok, c)
    return ok


def packed(tiles, width, side):
    k = SIDE // width
    rows, _, c = tiles.shape
    grouped = tiles.reshape(rows // k, k, SIDE, c)
    sub = lax.broadcasted_iota(jnp.int32, (rows // k, SIDE, c), 1)
    total = None
    for i in range(k):
        shift = (i * width - (0 if side == 0 else SIDE - width)) % SIDE
        piece = grouped[:, i]
        if shift:
            piece = pltpu.roll(piece, shift, 1)
        total = piece if total is None else jnp.where(sub >= i * width, piece, total)
    return total


def unpacked(tiles, width, side):
    k = SIDE // width
    count, _, c = tiles.shape
    pieces = []
    for i in range(k):
        shift = ((0 if side == 0 else SIDE - width) - i * width) % SIDE
        pieces.append(pltpu.roll(tiles, shift, 1) if shift else tiles)
    return jnp.stack(pieces, axis=1).reshape(count * k, SIDE, c)


def injected(p, t, weight):
    f = jnp.maximum(p, 0.0)
    g = jnp.maximum(t, 0.0)
    rinv = lax.rsqrt(jnp.mean(f * f, axis=-1, keepdims=True) + EPSILON)
    sinv = lax.rsqrt(jnp.mean(g * g, axis=-1, keepdims=True) + EPSILON)
    u = f * rinv
    e = weight * (u - g * sinv)
    return (e - u * jnp.mean(e * u, axis=-1, keepdims=True)) * rinv


def shifted_sum(z, n):
    length = z.shape[0]
    return pltpu.roll(z[:, :n], length - 1, 0) + z[:, n : 2 * n] + pltpu.roll(z[:, 2 * n :], 1, 0)


def conv_rows(x, w, first, rows, stride, n):
    length = rows * stride + 32
    start = first * stride - 16
    parts = [x[pl.ds(pl.multiple_of(start + (1 - dy) * stride, 16), length), :] for dy in range(3)]
    z = jnp.dot(jnp.concatenate(parts, axis=1), w[...], preferred_element_type=F32)
    return shifted_sum(z, n)[16 : 16 + rows * stride]


def body_kernel(axes, counts, shapes, *refs):
    (relu33, target33, relu32, relu31, relu22, target22, relu21,
     pool1, pool2, lin2, lin3, k21, k22, k31, k32, k33, out) = refs[:17]
    scratch = refs[17:]
    inputs = (None, relu32, relu31, relu22, target22, relu21)
    p33, t33 = scratch[:2]
    bufs = (None,) + tuple(scratch[2:7])
    sides, side_in, corner_in = scratch[7:13], scratch[13:19], scratch[19:25]
    (x33, x32, x31, x22, x21, w33, w32, w31, w22, w21, k21v, p1, p2, pedge, prow, pcol, pcor, upy, upp, yt, tmp, res,
     own_sem, w_sem, misc_sem, seed_send, seed_recv, send_sem, recv_sem, out_sem) = scratch[25:]
    n = 6
    off = [OFF3, OFF3, OFF3, OFF2, OFF2, OFF2]
    h3, wd3, c3 = shapes[0]
    h2, wd2, c2 = shapes[3]
    s3, s2 = wd3 + 2 * SIDE, wd2 + 2 * SIDE

    def own(a):
        return pltpu.make_async_copy(
            inputs[a], bufs[a].at[off[a] : off[a] + shapes[a][0], 0 : shapes[a][1]], own_sem.at[a])

    def weights(i):
        k, w = ((k33, w33), (k32, w32), (k31, w31), (k22, w22))[i]
        o, cols = k.shape[0], k.shape[1] // 3
        return [pltpu.make_async_copy(k.at[:, dy * cols : (dy + 1) * cols], w.at[dy * o : (dy + 1) * o], w_sem.at[i, dy])
                for dy in range(3)]

    others = [pltpu.make_async_copy(src, dst, misc_sem.at[i])
              for i, (src, dst) in enumerate(((relu33, p33), (target33, t33), (pool2, p2), (pool1, p1), (k21, k21v)))]
    others[0].start()
    others[1].start()
    for a in (1, 2, 3, 4, 5):
        own(a).start()
    others[2].start()
    for i in range(4):
        for c in weights(i):
            c.start()
    others[4].start()
    others[3].start()

    me = tuple(lax.axis_index(axis) for axis in axes)

    def peer(d):
        return (me[0] + d[0], me[1] + d[1])

    barrier = pltpu.get_barrier_semaphore()
    for d in DIRS:
        @pl.when(reachable(axes, counts, d, 1))
        def _():
            pl.semaphore_signal(barrier, inc=1, device_id=peer(d), device_id_type=MESH)
    spans = [1 + jnp.minimum(m, 1) + jnp.minimum(c - 1 - m, 1) for m, c in zip(me, counts)]
    pl.semaphore_wait(barrier, spans[0] * spans[1] - 1)

    def remote(src, dst, ssem, rsem, d):
        return pltpu.make_async_remote_copy(
            src_ref=src, dst_ref=dst, send_sem=ssem, recv_sem=rsem, device_id=peer(d), device_id_type=MESH)

    def corner_tiles(a):
        k = SIDE // WIDTHS[a]
        return -(-ROWS[a] // k)

    def messages(a, k):
        d = DIRS[k]
        ssem, rsem = send_sem.at[a, k], recv_sem.at[a, k]
        if a == n:
            if d[1] == 0:
                return [remote(pedge.at[k], prow.at[k], ssem, rsem, d)]
            rows = {0: slice(0, h3), -1: slice(0, 8), 1: slice(h3 - 8, h3)}[d[0]]
            lanes = slice(0, 128) if d[1] < 0 else slice((wd3 - 1) * 128, wd3 * 128)
            dst = pcol.at[k - 2] if d[0] == 0 else pcor.at[k - 4]
            return [remote(pool2.at[rows, lanes], dst, ssem, rsem, d)]
        if d[1] == 0:
            h, rows = ROWS[a], shapes[a][0]
            first, land = (0, rows) if d[0] < 0 else (rows - h, -h)
            if a == 0:
                return [remote(x33.at[(OFF3 + first + q) * s3 : (OFF3 + first + q) * s3 + wd3],
                               x33.at[(OFF3 + land + q) * s3 : (OFF3 + land + q) * s3 + wd3],
                               seed_send.at[k, q], seed_recv.at[k, q], d) for q in range(h)]
            return [remote(inputs[a].at[first : first + h],
                           bufs[a].at[off[a] + land : off[a] + land + h, 0 : shapes[a][1]], ssem, rsem, d)]
        side = 0 if d[1] < 0 else 1
        if d[0] == 0:
            return [remote(sides[a].at[side], side_in[a].at[side], ssem, rsem, d)]
        tiles, total = corner_tiles(a), sides[a].shape[1]
        first = 0 if d[0] < 0 else total - tiles
        return [remote(sides[a].at[side, first : first + tiles], corner_in[a].at[k - 4], ssem, rsem, d)]

    def send(a, ks):
        for k in ks:
            @pl.when(reachable(axes, counts, DIRS[k], 1))
            def _():
                for c in messages(a, k):
                    c.start()

    def put(a, row, slot, tiles):
        count = tiles.shape[0]
        tiles = tiles.astype(BF16)
        if a == 0:
            for q in range(count):
                at = (OFF3 + row + q) * s3 + slot
                x33[at : at + SIDE, :] = tiles[q]
        else:
            bufs[a][off[a] + row : off[a] + row + count, slot : slot + SIDE, :] = tiles

    def receive(a):
        h, (rows, cols, c) = ROWS[a], shapes[a]
        for k in range(8):
            d = DIRS[k]
            first, count = {0: (0, rows), -1: (rows, h), 1: (-h, h)}[d[0]]
            side = 0 if d[1] < 0 else 1
            slot = cols if side == 0 else cols + SIDE

            @pl.when(reachable(axes, counts, d, -1))
            def _():
                for m in messages(a, k):
                    m.wait_recv()
                if d[1]:
                    tiles = side_in[a][side] if d[0] == 0 else corner_in[a][k - 4]
                    spread = unpacked(tiles.astype(F32), WIDTHS[a], side)
                    spread = spread[:count] if d[0] <= 0 else spread[spread.shape[0] - count :]
                    put(a, first - side, slot, spread)

            if a != 4:
                @pl.when(jnp.logical_not(reachable(axes, counts, d, -1)))
                def _():
                    if d[1]:
                        put(a, first - side, slot, jnp.zeros((count, SIDE, c), F32))
                    elif a == 0:
                        for q in range(count):
                            x33[(OFF3 + first + q) * s3 : (OFF3 + first + q) * s3 + wd3, :] = jnp.zeros((wd3, c), BF16)
                    else:
                        bufs[a][off[a] + first : off[a] + first + count, 0:cols, :] = jnp.zeros((count, cols, c), BF16)

    def pack(a, side):
        rows, cols, c = shapes[a]
        at = 0 if side == 0 else cols - SIDE
        if a == 0:
            tiles = jnp.stack([x33[(OFF3 + q) * s3 + at : (OFF3 + q) * s3 + at + SIDE, :] for q in range(rows)])
        else:
            tiles = bufs[a][off[a] : off[a] + rows, at : at + SIDE, :]
        sides[a][side] = packed(tiles.astype(F32), WIDTHS[a], side).astype(BF16)

    weight3 = 2.0 * lin3[...]
    weight2 = 2.0 * lin2[...]
    others[0].wait()
    others[1].wait()

    @pl.loop(0, h3 // 2)
    def _(i):
        for q in range(2):
            p = p33[2 * i + q].astype(F32)
            t = t33[2 * i + q].astype(F32)
            seed = jnp.where(p > 0, injected(p, t, weight3), 0.0).astype(BF16)
            x33[pl.ds(pl.multiple_of((OFF3 + 2 * i + q) * s3, 16), wd3), :] = seed

    send(0, (0, 1))
    pack(0, 0)
    pack(0, 1)
    send(0, range(2, 8))
    for a in (1, 2, 3, 4, 5):
        send(a, (0, 1))
        own(a).wait()
        pack(a, 0)
        pack(a, 1)
        send(a, range(2, 8))
        if a == 2:
            others[2].wait()
            for j in range(wd3):
                pedge[0, j : j + 1, :] = p2[0:1, j * 128 : (j + 1) * 128]
                pedge[1, j : j + 1, :] = p2[h3 - 1 : h3, j * 128 : (j + 1) * 128]
            send(n, range(8))

    def masked_conv(x, w, p, y, first, rows, steps, stride, channels):
        @pl.loop(0, steps)
        def _(i):
            at = first + i * rows
            o = conv_rows(x, w, at, rows, stride, channels)
            pre = p[pl.ds(at, rows)].reshape(rows * stride, channels).astype(F32)
            y[pl.ds(pl.multiple_of(at * stride, 16), rows * stride), :] = jnp.where(pre > 0, o, 0.0).astype(BF16)

    for j in range(wd3):
        for i0 in range(0, h3, 8):
            blk = p2[i0 : i0 + 8, j * 128 : (j + 1) * 128]
            for b in range(2):
                upp[pl.ds((OFFU + i0) * s2 + 2 * j + b, 8, stride=s2), :] = blk
    others[4].wait()
    for tap in range(9):
        dy, dx = tap // 3, tap % 3
        rows = k21v[tap * 64 : (tap + 1) * 64, :].astype(F32)
        w21[dy * c2 : (dy + 1) * c2, dx * 128 : (dx + 1) * 128] = jnp.concatenate([rows, rows], axis=0).T.astype(BF16)
    receive(0)
    for c in weights(0):
        c.wait()
    receive(1)
    masked_conv(x33, w33, bufs[1], x32, OFF3 - 4, (h3 + 8) // 3, 3, s3, c3)
    receive(2)
    for c in weights(1):
        c.wait()
    masked_conv(x32, w32, bufs[2], x31, OFF3 - 3, (h3 + 5) // 3, 3, s3, c3)

    for k in range(8):
        @pl.when(reachable(axes, counts, DIRS[k], -1))
        def _():
            for m in messages(n, k):
                m.wait_recv()
    for b in range(2):
        upp[pl.ds((OFFU + h3) * s2 + b, wd3, stride=2), :] = prow[0]
        upp[pl.ds((OFFU - 1) * s2 + b, wd3, stride=2), :] = prow[1]
        for i0 in range(0, h3, 8):
            upp[pl.ds((OFFU + i0) * s2 + wd2 + b, 8, stride=s2), :] = pcol[0, i0 : i0 + 8]
            upp[pl.ds((OFFU + i0) * s2 + s2 - 2 + b, 8, stride=s2), :] = pcol[1, i0 : i0 + 8]
        upp[(OFFU + h3) * s2 + wd2 + b : (OFFU + h3) * s2 + wd2 + b + 1, :] = pcor[0, 0:1]
        upp[(OFFU + h3) * s2 + s2 - 2 + b : (OFFU + h3) * s2 + s2 - 2 + b + 1, :] = pcor[1, 0:1]
        upp[(OFFU - 1) * s2 + wd2 + b : (OFFU - 1) * s2 + wd2 + b + 1, :] = pcor[2, 7:8]
        upp[(OFFU - 1) * s2 + s2 - 2 + b : (OFFU - 1) * s2 + s2 - 2 + b + 1, :] = pcor[3, 7:8]

    for c in weights(2):
        c.wait()
    rows31 = (h3 + 4) // 4

    @pl.loop(0, 4)
    def _(i):
        o = conv_rows(x31, w31, OFF3 - 2 + i * rows31, rows31, s3, c2)
        for q in range(rows31):
            row = i * rows31 + q
            base = row * s2
            y = o[q * s3 : (q + 1) * s3]
            for b in range(2):
                upy[pl.ds(base + b, wd3, stride=2), :] = y[:wd3]
                upy[pl.ds(base + wd2 + b, 4, stride=2), :] = y[wd3 : wd3 + 4]
                upy[pl.ds(base + s2 + s2 - 8 + b, 4, stride=2), :] = y[s3 - 4 :]

    receive(3)
    receive(4)
    main = s2 - 8
    par = lax.broadcasted_iota(jnp.int32, (s2, 128), 0) % 2

    @pl.loop(0, h2 + 5)
    def _(i):
        for_row = i + OFF2 - 3
        r0 = (i + 1) // 2 + OFFU - 2
        a0 = (i + 1) % 2
        r1 = (i + 2) // 2 + OFFU - 2
        a1 = (i + 2) % 2
        at0 = pl.multiple_of(r0 * s2, 8)
        at1 = pl.multiple_of(r1 * s2 + main, 8)
        y = jnp.concatenate([upy[pl.ds(at0, main), :], upy[pl.ds(at1, 8), :]], axis=0)
        m = jnp.concatenate([upp[pl.ds(at0, main), :] - 2 * a0, upp[pl.ds(at1, 8), :] - 2 * a1], axis=0)
        p = bufs[3][for_row].astype(F32)
        t = bufs[4][for_row].astype(F32)
        arriving = jnp.where(m == par, y, 0.0) + injected(p, t, weight2)
        x22[pl.ds(pl.multiple_of(for_row * s2, 16), s2), :] = jnp.where(p > 0, arriving, 0.0).astype(BF16)

    receive(5)
    for c in weights(3):
        c.wait()
    masked_conv(x22, w22, bufs[5], x21, OFF2 - 2, (h2 + 3) // 5, 5, s2, c2)

    rows21 = 8

    @pl.loop(0, h2 // rows21)
    def _(i):
        o = conv_rows(x21, w21, OFF2 + i * rows21, rows21, s2, 128)
        for q in range(rows21):
            for j0 in range(0, wd2, 8):
                y = o[q * s2 + j0 : q * s2 + j0 + 8]
                for a in range(2):
                    yt[pl.ds(j0 * 2 * h2 + 2 * (i * rows21 + q) + a, 8, stride=2 * h2), :] = y

    others[3].wait()
    lane_low = lax.broadcasted_iota(jnp.int32, (2 * h2, 128), 1) < 64
    want = (lax.broadcasted_iota(jnp.int32, (2 * h2, 128), 0) % 2) * 2 + jnp.where(lane_low, 0, 1)

    @pl.loop(0, wd2 // 2)
    def _(g):
        lanes = pl.ds(pl.multiple_of(g * 128, 128), 128)
        blk = p1[:, lanes]
        for a in range(2):
            tmp[pl.ds(a, h2, stride=2), :] = blk
        m = tmp[...]
        turned = pltpu.roll(m, 64, 1)
        for e in range(2):
            y = yt[pl.ds(pl.multiple_of((2 * g + e) * 2 * h2, 8), 2 * h2), :]
            sel = jnp.where(lane_low, m, turned) if e == 0 else jnp.where(lane_low, turned, m)
            res[:, pl.ds(pl.multiple_of((2 * g + e) * 128, 128), 128)] = jnp.where(sel == want, y, 0.0).astype(BF16)

    done = pltpu.make_async_copy(res, out, out_sem)
    done.start()
    for a in range(n + 1):
        for k in range(8):
            @pl.when(reachable(axes, counts, DIRS[k], 1))
            def _():
                for m in messages(a, k):
                    m.wait_send()
    done.wait()


def shards(axes, counts, relu21, relu22, relu31, relu32, relu33, target22, target33, pool1, pool2, lin2, lin3,
           k21, k22, k31, k32, k33):
    tensors = (relu33, target33, relu32, relu31, relu22, target22, relu21)
    shapes = tuple(t.shape for t in (relu33, relu32, relu31, relu22, target22, relu21))
    h3, wd3, c3 = relu33.shape
    h2, wd2, c2 = relu22.shape
    s3, s2 = wd3 + 2 * SIDE, wd2 + 2 * SIDE
    anywhere = pl.BlockSpec(memory_space=pl.ANY)
    vmem = pl.BlockSpec(memory_space=pltpu.VMEM)
    rows3, rows2 = h3 + 2 * OFF3, h2 + 2 * OFF2
    per = [SIDE // w for w in WIDTHS]
    scratch = [pltpu.VMEM((h3, wd3, c3), BF16)] * 2
    scratch += [pltpu.VMEM((rows3, s3, c3), BF16)] * 2 + [pltpu.VMEM((rows2, s2, c2), BF16)] * 3
    scratch += [pltpu.VMEM((2, s[0] // k, SIDE, s[2]), BF16) for s, k in zip(shapes, per)] * 2
    scratch += [pltpu.VMEM((4, -(-r // k), SIDE, s[2]), BF16) for s, k, r in zip(shapes, per, ROWS)]
    scratch += [pltpu.VMEM((rows3 * s3, c3), BF16)] * 3 + [pltpu.VMEM((rows2 * s2, c2), BF16)] * 2
    scratch += [pltpu.VMEM((3 * k.shape[0], k.shape[1] // 3), BF16) for k in (k33, k32, k31, k22)]
    scratch += [
        pltpu.VMEM((3 * c2, 384), BF16),
        pltpu.VMEM(k21.shape[::-1], BF16),
        pltpu.VMEM(pool1.shape, jnp.int32),
        pltpu.VMEM(pool2.shape, jnp.int32),
        pltpu.VMEM((2, wd3, 128), jnp.int32),
        pltpu.VMEM((2, wd3, 128), jnp.int32),
        pltpu.VMEM((2, h3, 128), jnp.int32),
        pltpu.VMEM((4, 8, 128), jnp.int32),
        pltpu.VMEM(((h3 + 2 * OFFU + 1) * s2, 128), F32),
        pltpu.VMEM(((h3 + 2 * OFFU + 1) * s2, 128), jnp.int32),
        pltpu.VMEM((wd2 * 2 * h2, 128), F32),
        pltpu.VMEM((2 * h2, 128), jnp.int32),
        pltpu.VMEM((2 * h2, wd2 * 128), BF16),
        pltpu.SemaphoreType.DMA((6,)),
        pltpu.SemaphoreType.DMA((4, 3)),
        pltpu.SemaphoreType.DMA((5,)),
        pltpu.SemaphoreType.DMA((2, 4)),
        pltpu.SemaphoreType.DMA((2, 4)),
        pltpu.SemaphoreType.DMA((7, 8)),
        pltpu.SemaphoreType.DMA((7, 8)),
        pltpu.SemaphoreType.DMA(()),
    ]
    return pl.pallas_call(
        functools.partial(body_kernel, axes, counts, shapes),
        out_shape=jax.ShapeDtypeStruct((2 * h2, wd2 * 128), BF16),
        in_specs=[anywhere] * 9 + [vmem] * 2 + [anywhere] * 5,
        out_specs=anywhere,
        scratch_shapes=scratch,
        compiler_params=pltpu.CompilerParams(
            vmem_limit_bytes=56 * 1024 * 1024, collective_id=0, has_side_effects=True),
        name="body",
    )(*tensors, pool1, pool2, lin2.reshape(1, c2), lin3.reshape(1, c3), k21.T, k22, k31, k32, k33)


def solution(mesh):
    axes = ("row", "col")
    counts = tuple(mesh.shape[a] for a in axes)
    cells = P("row", "col", None)
    in_specs = (cells,) * 7 + (P("row", "col"),) * 2 + (P(),) * 7
    return jax.shard_map(functools.partial(shards, axes, counts), mesh=mesh, in_specs=in_specs,
                         out_specs=P("row", "col"), check_vma=False)
```

```python
import functools

import jax
import jax.numpy as jnp
from jax import lax
from jax.experimental import pallas as pl
from jax.experimental.pallas import tpu as pltpu
from jax.sharding import PartitionSpec as P

EPSILON = 1e-06
MESH = pl.DeviceIdType.MESH
F32 = jnp.float32
BF16 = jnp.bfloat16
SIDE = 8
OFF3 = 6
OFF2 = 4
OFFU = 2
DIRS = ((-1, 0), (1, 0), (0, -1), (0, 1), (-1, -1), (-1, 1), (1, -1), (1, 1))


WIDTHS = (4, 4, 2, 2, 2, 1)
ROWS = (4, 3, 2, 2, 2, 1)


def reachable(axes, counts, d, sign):
    checks = []
    for axis, count, step in zip(axes, counts, d):
        if step:
            target = lax.axis_index(axis) + sign * step
            checks.append(target >= 0 if sign * step < 0 else target < count)
    ok = checks[0]
    for c in checks[1:]:
        ok = jnp.logical_and(ok, c)
    return ok


def packed(tiles, width, side):
    k = SIDE // width
    rows, _, c = tiles.shape
    grouped = tiles.reshape(rows // k, k, SIDE, c)
    sub = lax.broadcasted_iota(jnp.int32, (rows // k, SIDE, c), 1)
    total = None
    for i in range(k):
        shift = (i * width - (0 if side == 0 else SIDE - width)) % SIDE
        piece = grouped[:, i]
        if shift:
            piece = pltpu.roll(piece, shift, 1)
        total = piece if total is None else jnp.where(sub >= i * width, piece, total)
    return total


def unpacked(tiles, width, side):
    k = SIDE // width
    count, _, c = tiles.shape
    pieces = []
    for i in range(k):
        shift = ((0 if side == 0 else SIDE - width) - i * width) % SIDE
        pieces.append(pltpu.roll(tiles, shift, 1) if shift else tiles)
    return jnp.stack(pieces, axis=1).reshape(count * k, SIDE, c)


def injected(p, t, weight):
    f = jnp.maximum(p, 0.0)
    g = jnp.maximum(t, 0.0)
    rinv = lax.rsqrt(jnp.mean(f * f, axis=-1, keepdims=True) + EPSILON)
    sinv = lax.rsqrt(jnp.mean(g * g, axis=-1, keepdims=True) + EPSILON)
    u = f * rinv
    e = weight * (u - g * sinv)
    return (e - u * jnp.mean(e * u, axis=-1, keepdims=True)) * rinv


def shifted_sum(z, n):
    length = z.shape[0]
    return pltpu.roll(z[:, :n], length - 1, 0) + z[:, n : 2 * n] + pltpu.roll(z[:, 2 * n :], 1, 0)


def conv_rows(x, w, first, rows, stride, n):
    length = rows * stride + 32
    start = first * stride - 16
    parts = [x[pl.ds(pl.multiple_of(start + (1 - dy) * stride, 16), length), :] for dy in range(3)]
    z = jnp.dot(jnp.concatenate(parts, axis=1), w[...], preferred_element_type=F32)
    return shifted_sum(z, n)[16 : 16 + rows * stride]


def body_kernel(axes, counts, shapes, *refs):
    (relu33, target33, relu32, relu31, relu22, target22, relu21,
     pool1, pool2, lin2, lin3, k21, k22, k31, k32, k33, out) = refs[:17]
    scratch = refs[17:]
    inputs = (None, relu32, relu31, relu22, target22, relu21)
    p33, t33 = scratch[:2]
    bufs = (None,) + tuple(scratch[2:7])
    sides, side_in, corner_in = scratch[7:13], scratch[13:19], scratch[19:25]
    (x33, x32, x31, x22, x21, w33, w32, w31, w22, w21, k21v, p1, p2, pedge, prow, pcol, pcor, upy, upp, yt, twice, injs, res,
     own_sem, w_sem, misc_sem, seed_send, seed_recv, send_sem, recv_sem, out_sem) = scratch[25:]
    n = 6
    off = [OFF3, OFF3, OFF3, OFF2, OFF2, OFF2]
    h3, wd3, c3 = shapes[0]
    h2, wd2, c2 = shapes[3]
    s3, s2 = wd3 + 2 * SIDE, wd2 + 2 * SIDE

    def own(a):
        return pltpu.make_async_copy(
            inputs[a], bufs[a].at[off[a] : off[a] + shapes[a][0], 0 : shapes[a][1]], own_sem.at[a])

    def weights(i):
        k, w = ((k33, w33), (k32, w32), (k31, w31), (k22, w22))[i]
        o, cols = k.shape[0], k.shape[1] // 3
        return [pltpu.make_async_copy(k.at[:, dy * cols : (dy + 1) * cols], w.at[dy * o : (dy + 1) * o], w_sem.at[i, dy])
                for dy in range(3)]

    others = [pltpu.make_async_copy(src, dst, misc_sem.at[i])
              for i, (src, dst) in enumerate(((relu33, p33), (target33, t33), (pool2, p2), (pool1, p1), (k21, k21v)))]
    others[0].start()
    others[1].start()
    for a in (1, 2, 3, 4, 5):
        own(a).start()
    others[2].start()
    for i in range(4):
        for c in weights(i):
            c.start()
    others[4].start()
    others[3].start()

    me = tuple(lax.axis_index(axis) for axis in axes)

    def peer(d):
        return (me[0] + d[0], me[1] + d[1])

    barrier = pltpu.get_barrier_semaphore()
    for d in DIRS:
        @pl.when(reachable(axes, counts, d, 1))
        def _():
            pl.semaphore_signal(barrier, inc=1, device_id=peer(d), device_id_type=MESH)
    spans = [1 + jnp.minimum(m, 1) + jnp.minimum(c - 1 - m, 1) for m, c in zip(me, counts)]
    pl.semaphore_wait(barrier, spans[0] * spans[1] - 1)

    def remote(src, dst, ssem, rsem, d):
        return pltpu.make_async_remote_copy(
            src_ref=src, dst_ref=dst, send_sem=ssem, recv_sem=rsem, device_id=peer(d), device_id_type=MESH)

    def corner_tiles(a):
        k = SIDE // WIDTHS[a]
        return -(-ROWS[a] // k)

    def messages(a, k):
        d = DIRS[k]
        ssem, rsem = send_sem.at[a, k], recv_sem.at[a, k]
        if a == n:
            if d[1] == 0:
                return [remote(pedge.at[k], prow.at[k], ssem, rsem, d)]
            rows = {0: slice(0, h3), -1: slice(0, 8), 1: slice(h3 - 8, h3)}[d[0]]
            lanes = slice(0, 128) if d[1] < 0 else slice((wd3 - 1) * 128, wd3 * 128)
            dst = pcol.at[k - 2] if d[0] == 0 else pcor.at[k - 4]
            return [remote(pool2.at[rows, lanes], dst, ssem, rsem, d)]
        if d[1] == 0:
            h, rows = ROWS[a], shapes[a][0]
            first, land = (0, rows) if d[0] < 0 else (rows - h, -h)
            if a == 0:
                return [remote(x33.at[(OFF3 + first + q) * s3 : (OFF3 + first + q) * s3 + wd3],
                               x33.at[(OFF3 + land + q) * s3 : (OFF3 + land + q) * s3 + wd3],
                               seed_send.at[k, q], seed_recv.at[k, q], d) for q in range(h)]
            return [remote(inputs[a].at[first : first + h],
                           bufs[a].at[off[a] + land : off[a] + land + h, 0 : shapes[a][1]], ssem, rsem, d)]
        side = 0 if d[1] < 0 else 1
        if d[0] == 0:
            return [remote(sides[a].at[side], side_in[a].at[side], ssem, rsem, d)]
        tiles, total = corner_tiles(a), sides[a].shape[1]
        first = 0 if d[0] < 0 else total - tiles
        return [remote(sides[a].at[side, first : first + tiles], corner_in[a].at[k - 4], ssem, rsem, d)]

    def send(a, ks):
        for k in ks:
            @pl.when(reachable(axes, counts, DIRS[k], 1))
            def _():
                for c in messages(a, k):
                    c.start()

    def put(a, row, slot, tiles):
        count = tiles.shape[0]
        tiles = tiles.astype(BF16)
        if a == 0:
            for q in range(count):
                at = (OFF3 + row + q) * s3 + slot
                x33[at : at + SIDE, :] = tiles[q]
        else:
            bufs[a][off[a] + row : off[a] + row + count, slot : slot + SIDE, :] = tiles

    def receive(a):
        h, (rows, cols, c) = ROWS[a], shapes[a]
        for k in range(8):
            d = DIRS[k]
            first, count = {0: (0, rows), -1: (rows, h), 1: (-h, h)}[d[0]]
            side = 0 if d[1] < 0 else 1
            slot = cols if side == 0 else cols + SIDE

            @pl.when(reachable(axes, counts, d, -1))
            def _():
                for m in messages(a, k):
                    m.wait_recv()
                if d[1]:
                    tiles = side_in[a][side] if d[0] == 0 else corner_in[a][k - 4]
                    spread = unpacked(tiles.astype(F32), WIDTHS[a], side)
                    spread = spread[:count] if d[0] <= 0 else spread[spread.shape[0] - count :]
                    put(a, first - side, slot, spread)

            if a != 4:
                @pl.when(jnp.logical_not(reachable(axes, counts, d, -1)))
                def _():
                    if d[1]:
                        put(a, first - side, slot, jnp.zeros((count, SIDE, c), F32))
                    elif a == 0:
                        for q in range(count):
                            x33[(OFF3 + first + q) * s3 : (OFF3 + first + q) * s3 + wd3, :] = jnp.zeros((wd3, c), BF16)
                    else:
                        bufs[a][off[a] + first : off[a] + first + count, 0:cols, :] = jnp.zeros((count, cols, c), BF16)

    def pack(a, side):
        rows, cols, c = shapes[a]
        at = 0 if side == 0 else cols - SIDE
        if a == 0:
            tiles = jnp.stack([x33[(OFF3 + q) * s3 + at : (OFF3 + q) * s3 + at + SIDE, :] for q in range(rows)])
        else:
            tiles = bufs[a][off[a] : off[a] + rows, at : at + SIDE, :]
        sides[a][side] = packed(tiles.astype(F32), WIDTHS[a], side).astype(BF16)

    weight3 = 2.0 * lin3[...]
    weight2 = 2.0 * lin2[...]
    others[0].wait()
    others[1].wait()

    @pl.loop(0, h3 // 2)
    def _(i):
        for q in range(2):
            p = p33[2 * i + q].astype(F32)
            t = t33[2 * i + q].astype(F32)
            seed = jnp.where(p > 0, injected(p, t, weight3), 0.0).astype(BF16)
            x33[pl.ds(pl.multiple_of((OFF3 + 2 * i + q) * s3, 16), wd3), :] = seed

    send(0, (0, 1))
    pack(0, 0)
    pack(0, 1)
    send(0, range(2, 8))
    for a in (1, 2, 3, 4, 5):
        send(a, (0, 1))
        own(a).wait()
        pack(a, 0)
        pack(a, 1)
        send(a, range(2, 8))
        if a == 2:
            others[2].wait()
            for j in range(wd3):
                pedge[0, j : j + 1, :] = p2[0:1, j * 128 : (j + 1) * 128]
                pedge[1, j : j + 1, :] = p2[h3 - 1 : h3, j * 128 : (j + 1) * 128]
            send(n, range(8))

    def masked_conv(x, w, p, y, first, rows, steps, stride, channels):
        @pl.loop(0, steps)
        def _(i):
            at = first + i * rows
            o = conv_rows(x, w, at, rows, stride, channels)
            pre = p[pl.ds(at, rows)].reshape(rows * stride, channels).astype(F32)
            y[pl.ds(pl.multiple_of(at * stride, 16), rows * stride), :] = jnp.where(pre > 0, o, 0.0).astype(BF16)

    for j in range(wd3):
        for i0 in range(0, h3, 8):
            blk = p2[i0 : i0 + 8, j * 128 : (j + 1) * 128]
            for b in range(2):
                upp[pl.ds((OFFU + i0) * s2 + 2 * j + b, 8, stride=s2), :] = blk
    others[4].wait()
    for tap in range(9):
        dy, dx = tap // 3, tap % 3
        rows = k21v[tap * 64 : (tap + 1) * 64, :].astype(F32)
        w21[dy * c2 : (dy + 1) * c2, dx * 128 : (dx + 1) * 128] = jnp.concatenate([rows, rows], axis=0).T.astype(BF16)
    rows2 = bufs[3].shape[0]

    def inject_at(row, count, slot, width):
        p = bufs[3][pl.ds(row, count), slot : slot + width, :].reshape(count * width, c2).astype(F32)
        t = bufs[4][pl.ds(row, count), slot : slot + width, :].reshape(count * width, c2).astype(F32)
        value = injected(p, t, weight2)
        for q in range(count):
            injs[pl.ds(pl.multiple_of((row + q) * s2 + slot, 16), width), :] = value[q * width : (q + 1) * width]

    @pl.loop(0, h2 // 4)
    def _(i):
        inject_at(OFF2 + 4 * i, 4, 0, wd2)

    others[3].wait()

    @pl.loop(0, wd2 // 2)
    def _(g):
        blk = p1[:, pl.ds(pl.multiple_of(g * 128, 128), 128)]
        for a in range(2):
            twice[pl.ds(g * 2 * h2 + a, h2, stride=2), :] = blk

    receive(0)
    for c in weights(0):
        c.wait()
    receive(1)
    masked_conv(x33, w33, bufs[1], x32, OFF3 - 4, (h3 + 8) // 3, 3, s3, c3)
    receive(2)
    for c in weights(1):
        c.wait()
    masked_conv(x32, w32, bufs[2], x31, OFF3 - 3, (h3 + 5) // 3, 3, s3, c3)

    for k in range(8):
        @pl.when(reachable(axes, counts, DIRS[k], -1))
        def _():
            for m in messages(n, k):
                m.wait_recv()
    for b in range(2):
        upp[pl.ds((OFFU + h3) * s2 + b, wd3, stride=2), :] = prow[0]
        upp[pl.ds((OFFU - 1) * s2 + b, wd3, stride=2), :] = prow[1]
        for i0 in range(0, h3, 8):
            upp[pl.ds((OFFU + i0) * s2 + wd2 + b, 8, stride=s2), :] = pcol[0, i0 : i0 + 8]
            upp[pl.ds((OFFU + i0) * s2 + s2 - 2 + b, 8, stride=s2), :] = pcol[1, i0 : i0 + 8]
        upp[(OFFU + h3) * s2 + wd2 + b : (OFFU + h3) * s2 + wd2 + b + 1, :] = pcor[0, 0:1]
        upp[(OFFU + h3) * s2 + s2 - 2 + b : (OFFU + h3) * s2 + s2 - 2 + b + 1, :] = pcor[1, 0:1]
        upp[(OFFU - 1) * s2 + wd2 + b : (OFFU - 1) * s2 + wd2 + b + 1, :] = pcor[2, 7:8]
        upp[(OFFU - 1) * s2 + s2 - 2 + b : (OFFU - 1) * s2 + s2 - 2 + b + 1, :] = pcor[3, 7:8]

    for c in weights(2):
        c.wait()
    rows31 = (h3 + 4) // 4

    @pl.loop(0, 4)
    def _(i):
        o = conv_rows(x31, w31, OFF3 - 2 + i * rows31, rows31, s3, c2)
        for q in range(rows31):
            row = i * rows31 + q
            base = row * s2
            y = o[q * s3 : (q + 1) * s3]
            for b in range(2):
                upy[pl.ds(base + b, wd3, stride=2), :] = y[:wd3]
                upy[pl.ds(base + wd2 + b, 4, stride=2), :] = y[wd3 : wd3 + 4]
                upy[pl.ds(base + s2 + s2 - 8 + b, 4, stride=2), :] = y[s3 - 4 :]

    receive(3)
    receive(4)
    for q in range(0, rows2, SIDE):
        inject_at(q, SIDE, wd2, 2 * SIDE)
    inject_at(OFF2 - 2, 2, 0, wd2)
    inject_at(OFF2 + h2, 2, 0, wd2)
    main = s2 - 8
    par = lax.broadcasted_iota(jnp.int32, (s2, 128), 0) % 2

    @pl.loop(0, (h2 + 6) // 2)
    def _(half):
        for i in (2 * half, 2 * half + 1):
            for_row = i + OFF2 - 3
            r0 = (i + 1) // 2 + OFFU - 2
            a0 = (i + 1) % 2
            r1 = (i + 2) // 2 + OFFU - 2
            a1 = (i + 2) % 2
            at0 = pl.multiple_of(r0 * s2, 8)
            at1 = pl.multiple_of(r1 * s2 + main, 8)
            here = pl.ds(pl.multiple_of(for_row * s2, 16), s2)
            y = jnp.concatenate([upy[pl.ds(at0, main), :], upy[pl.ds(at1, 8), :]], axis=0)
            m = jnp.concatenate([upp[pl.ds(at0, main), :] - 2 * a0, upp[pl.ds(at1, 8), :] - 2 * a1], axis=0)
            p = bufs[3][for_row].astype(F32)
            arriving = jnp.where(m == par, y, 0.0) + injs[here, :]
            x22[here, :] = jnp.where(p > 0, arriving, 0.0).astype(BF16)

    receive(5)
    for c in weights(3):
        c.wait()
    masked_conv(x22, w22, bufs[5], x21, OFF2 - 2, (h2 + 3) // 5, 5, s2, c2)

    rows21 = 8

    @pl.loop(0, h2 // rows21)
    def _(i):
        o = conv_rows(x21, w21, OFF2 + i * rows21, rows21, s2, 128)
        for q in range(rows21):
            for j0 in range(0, wd2, 8):
                y = o[q * s2 + j0 : q * s2 + j0 + 8]
                for a in range(2):
                    yt[pl.ds(j0 * 2 * h2 + 2 * (i * rows21 + q) + a, 8, stride=2 * h2), :] = y

    lane_low = lax.broadcasted_iota(jnp.int32, (2 * h2, 128), 1) < 64
    want = (lax.broadcasted_iota(jnp.int32, (2 * h2, 128), 0) % 2) * 2 + jnp.where(lane_low, 0, 1)
    share = wd2 // 8
    parts = []
    for part in range(4):
        @pl.loop(0, share)
        def _(v):
            g = part * share + v
            m = twice[pl.ds(pl.multiple_of(g * 2 * h2, 8), 2 * h2), :]
            turned = pltpu.roll(m, 64, 1)
            for e in range(2):
                y = yt[pl.ds(pl.multiple_of((2 * g + e) * 2 * h2, 8), 2 * h2), :]
                sel = jnp.where(lane_low, m, turned) if e == 0 else jnp.where(lane_low, turned, m)
                res[:, pl.ds(pl.multiple_of((2 * g + e) * 128, 128), 128)] = jnp.where(sel == want, y, 0.0).astype(BF16)

        lanes = slice(part * share * 256, (part + 1) * share * 256)
        parts.append(pltpu.make_async_copy(res.at[:, lanes], out.at[:, lanes], out_sem.at[part]))
        parts[-1].start()
    for a in range(n + 1):
        for k in range(8):
            @pl.when(reachable(axes, counts, DIRS[k], 1))
            def _():
                for m in messages(a, k):
                    m.wait_send()
    for c in parts:
        c.wait()


def shards(axes, counts, relu21, relu22, relu31, relu32, relu33, target22, target33, pool1, pool2, lin2, lin3,
           k21, k22, k31, k32, k33):
    tensors = (relu33, target33, relu32, relu31, relu22, target22, relu21)
    shapes = tuple(t.shape for t in (relu33, relu32, relu31, relu22, target22, relu21))
    h3, wd3, c3 = relu33.shape
    h2, wd2, c2 = relu22.shape
    s3, s2 = wd3 + 2 * SIDE, wd2 + 2 * SIDE
    anywhere = pl.BlockSpec(memory_space=pl.ANY)
    vmem = pl.BlockSpec(memory_space=pltpu.VMEM)
    rows3, rows2 = h3 + 2 * OFF3, h2 + 2 * OFF2
    per = [SIDE // w for w in WIDTHS]
    scratch = [pltpu.VMEM((h3, wd3, c3), BF16)] * 2
    scratch += [pltpu.VMEM((rows3, s3, c3), BF16)] * 2 + [pltpu.VMEM((rows2, s2, c2), BF16)] * 3
    scratch += [pltpu.VMEM((2, s[0] // k, SIDE, s[2]), BF16) for s, k in zip(shapes, per)] * 2
    scratch += [pltpu.VMEM((4, -(-r // k), SIDE, s[2]), BF16) for s, k, r in zip(shapes, per, ROWS)]
    scratch += [pltpu.VMEM((rows3 * s3, c3), BF16)] * 3 + [pltpu.VMEM((rows2 * s2, c2), BF16)] * 2
    scratch += [pltpu.VMEM((3 * k.shape[0], k.shape[1] // 3), BF16) for k in (k33, k32, k31, k22)]
    scratch += [
        pltpu.VMEM((3 * c2, 384), BF16),
        pltpu.VMEM(k21.shape[::-1], BF16),
        pltpu.VMEM(pool1.shape, jnp.int32),
        pltpu.VMEM(pool2.shape, jnp.int32),
        pltpu.VMEM((2, wd3, 128), jnp.int32),
        pltpu.VMEM((2, wd3, 128), jnp.int32),
        pltpu.VMEM((2, h3, 128), jnp.int32),
        pltpu.VMEM((4, 8, 128), jnp.int32),
        pltpu.VMEM(((h3 + 2 * OFFU + 1) * s2, 128), F32),
        pltpu.VMEM(((h3 + 2 * OFFU + 1) * s2, 128), jnp.int32),
        pltpu.VMEM((wd2 * 2 * h2, 128), F32),
        pltpu.VMEM((wd2 * h2, 128), jnp.int32),
        pltpu.VMEM((rows2 * s2, c2), F32),
        pltpu.VMEM((2 * h2, wd2 * 128), BF16),
        pltpu.SemaphoreType.DMA((6,)),
        pltpu.SemaphoreType.DMA((4, 3)),
        pltpu.SemaphoreType.DMA((5,)),
        pltpu.SemaphoreType.DMA((2, 4)),
        pltpu.SemaphoreType.DMA((2, 4)),
        pltpu.SemaphoreType.DMA((7, 8)),
        pltpu.SemaphoreType.DMA((7, 8)),
        pltpu.SemaphoreType.DMA((4,)),
    ]
    return pl.pallas_call(
        functools.partial(body_kernel, axes, counts, shapes),
        out_shape=jax.ShapeDtypeStruct((2 * h2, wd2 * 128), BF16),
        in_specs=[anywhere] * 9 + [vmem] * 2 + [anywhere] * 5,
        out_specs=anywhere,
        scratch_shapes=scratch,
        compiler_params=pltpu.CompilerParams(
            vmem_limit_bytes=56 * 1024 * 1024, collective_id=0, has_side_effects=True),
        name="body",
    )(*tensors, pool1, pool2, lin2.reshape(1, c2), lin3.reshape(1, c3), k21.T, k22, k31, k32, k33)


def solution(mesh):
    axes = ("row", "col")
    counts = tuple(mesh.shape[a] for a in axes)
    cells = P("row", "col", None)
    in_specs = (cells,) * 7 + (P("row", "col"),) * 2 + (P(),) * 7
    return jax.shard_map(functools.partial(shards, axes, counts), mesh=mesh, in_specs=in_specs,
                         out_specs=P("row", "col"), check_vma=False)
```

```python
import functools

import jax
import jax.numpy as jnp
from jax import lax
from jax.experimental import pallas as pl
from jax.experimental.pallas import tpu as pltpu
from jax.sharding import PartitionSpec as P

EPSILON = 1e-06
MESH = pl.DeviceIdType.MESH
F32 = jnp.float32
BF16 = jnp.bfloat16
SIDE = 8
OFF3 = 6
OFF2 = 4
OFFU = 2
DIRS = ((-1, 0), (1, 0), (0, -1), (0, 1), (-1, -1), (-1, 1), (1, -1), (1, 1))


WIDTHS = (4, 4, 2, 2, 2, 1)
ROWS = (4, 3, 2, 2, 2, 1)


def reachable(axes, counts, d, sign):
    checks = []
    for axis, count, step in zip(axes, counts, d):
        if step:
            target = lax.axis_index(axis) + sign * step
            checks.append(target >= 0 if sign * step < 0 else target < count)
    ok = checks[0]
    for c in checks[1:]:
        ok = jnp.logical_and(ok, c)
    return ok


def packed(tiles, width, side):
    k = SIDE // width
    rows, _, c = tiles.shape
    grouped = tiles.reshape(rows // k, k, SIDE, c)
    sub = lax.broadcasted_iota(jnp.int32, (rows // k, SIDE, c), 1)
    total = None
    for i in range(k):
        shift = (i * width - (0 if side == 0 else SIDE - width)) % SIDE
        piece = grouped[:, i]
        if shift:
            piece = pltpu.roll(piece, shift, 1)
        total = piece if total is None else jnp.where(sub >= i * width, piece, total)
    return total


def unpacked(tiles, width, side):
    k = SIDE // width
    count, _, c = tiles.shape
    pieces = []
    for i in range(k):
        shift = ((0 if side == 0 else SIDE - width) - i * width) % SIDE
        pieces.append(pltpu.roll(tiles, shift, 1) if shift else tiles)
    return jnp.stack(pieces, axis=1).reshape(count * k, SIDE, c)


def injected(p, t, weight):
    f = jnp.maximum(p, 0.0)
    g = jnp.maximum(t, 0.0)
    rinv = lax.rsqrt(jnp.mean(f * f, axis=-1, keepdims=True) + EPSILON)
    sinv = lax.rsqrt(jnp.mean(g * g, axis=-1, keepdims=True) + EPSILON)
    u = f * rinv
    e = weight * (u - g * sinv)
    return (e - u * jnp.mean(e * u, axis=-1, keepdims=True)) * rinv


def shifted_sum(z, n):
    length = z.shape[0]
    return pltpu.roll(z[:, :n], length - 1, 0) + z[:, n : 2 * n] + pltpu.roll(z[:, 2 * n :], 1, 0)


def conv_rows(x, w, first, rows, stride, n):
    length = rows * stride + 32
    start = first * stride - 16
    parts = [x[pl.ds(pl.multiple_of(start + (1 - dy) * stride, 16), length), :] for dy in range(3)]
    z = jnp.dot(jnp.concatenate(parts, axis=1), w[...], preferred_element_type=F32)
    return shifted_sum(z, n)[16 : 16 + rows * stride]


def body_kernel(axes, counts, shapes, *refs):
    (relu33, target33, relu32, relu31, relu22, target22, relu21,
     pool1, pool2, lin2, lin3, k21, k22, k31, k32, k33, out) = refs[:17]
    scratch = refs[17:]
    inputs = (None, relu32, relu31, relu22, target22, relu21)
    p33, t33 = scratch[:2]
    bufs = (None,) + tuple(scratch[2:7])
    sides, side_in, corner_in = scratch[7:13], scratch[13:19], scratch[19:25]
    (x33, x32, x31, x22, x21, w33, w32, w31, w22, w21, k21v, p1, p2, pedge, prow, pcol, pcor, upy, upp, yt, twice, injs, res,
     own_sem, w_sem, misc_sem, seed_send, seed_recv, send_sem, recv_sem, out_sem) = scratch[25:]
    n = 6
    off = [OFF3, OFF3, OFF3, OFF2, OFF2, OFF2]
    h3, wd3, c3 = shapes[0]
    h2, wd2, c2 = shapes[3]
    s3, s2 = wd3 + 2 * SIDE, wd2 + 2 * SIDE

    def own(a):
        return pltpu.make_async_copy(
            inputs[a], bufs[a].at[off[a] : off[a] + shapes[a][0], 0 : shapes[a][1]], own_sem.at[a])

    def weights(i):
        k, w = ((k33, w33), (k32, w32), (k31, w31), (k22, w22))[i]
        o, cols = k.shape[0], k.shape[1] // 3
        return [pltpu.make_async_copy(k.at[:, dy * cols : (dy + 1) * cols], w.at[dy * o : (dy + 1) * o], w_sem.at[i, dy])
                for dy in range(3)]

    others = [pltpu.make_async_copy(src, dst, misc_sem.at[i])
              for i, (src, dst) in enumerate(((relu33, p33), (target33, t33), (pool2, p2), (pool1, p1), (k21, k21v)))]
    others[0].start()
    others[1].start()
    for a in (1, 2, 3, 4, 5):
        own(a).start()
    others[2].start()
    for i in range(4):
        for c in weights(i):
            c.start()
    others[4].start()
    others[3].start()

    me = tuple(lax.axis_index(axis) for axis in axes)

    def peer(d):
        return (me[0] + d[0], me[1] + d[1])

    barrier = pltpu.get_barrier_semaphore()
    for d in DIRS:
        @pl.when(reachable(axes, counts, d, 1))
        def _():
            pl.semaphore_signal(barrier, inc=1, device_id=peer(d), device_id_type=MESH)
    spans = [1 + jnp.minimum(m, 1) + jnp.minimum(c - 1 - m, 1) for m, c in zip(me, counts)]
    pl.semaphore_wait(barrier, spans[0] * spans[1] - 1)

    def remote(src, dst, ssem, rsem, d):
        return pltpu.make_async_remote_copy(
            src_ref=src, dst_ref=dst, send_sem=ssem, recv_sem=rsem, device_id=peer(d), device_id_type=MESH)

    def corner_tiles(a):
        k = SIDE // WIDTHS[a]
        return -(-ROWS[a] // k)

    def messages(a, k):
        d = DIRS[k]
        ssem, rsem = send_sem.at[a, k], recv_sem.at[a, k]
        if a == n:
            if d[1] == 0:
                return [remote(pedge.at[k], prow.at[k], ssem, rsem, d)]
            rows = {0: slice(0, h3), -1: slice(0, 8), 1: slice(h3 - 8, h3)}[d[0]]
            lanes = slice(0, 128) if d[1] < 0 else slice((wd3 - 1) * 128, wd3 * 128)
            dst = pcol.at[k - 2] if d[0] == 0 else pcor.at[k - 4]
            return [remote(pool2.at[rows, lanes], dst, ssem, rsem, d)]
        if d[1] == 0:
            h, rows = ROWS[a], shapes[a][0]
            first, land = (0, rows) if d[0] < 0 else (rows - h, -h)
            if a == 0:
                return [remote(x33.at[(OFF3 + first + q) * s3 : (OFF3 + first + q) * s3 + wd3],
                               x33.at[(OFF3 + land + q) * s3 : (OFF3 + land + q) * s3 + wd3],
                               seed_send.at[k, q], seed_recv.at[k, q], d) for q in range(h)]
            return [remote(inputs[a].at[first : first + h],
                           bufs[a].at[off[a] + land : off[a] + land + h, 0 : shapes[a][1]], ssem, rsem, d)]
        side = 0 if d[1] < 0 else 1
        if d[0] == 0:
            return [remote(sides[a].at[side], side_in[a].at[side], ssem, rsem, d)]
        tiles, total = corner_tiles(a), sides[a].shape[1]
        first = 0 if d[0] < 0 else total - tiles
        return [remote(sides[a].at[side, first : first + tiles], corner_in[a].at[k - 4], ssem, rsem, d)]

    def send(a, ks):
        for k in ks:
            @pl.when(reachable(axes, counts, DIRS[k], 1))
            def _():
                for c in messages(a, k):
                    c.start()

    def put(a, row, slot, tiles):
        count = tiles.shape[0]
        tiles = tiles.astype(BF16)
        if a == 0:
            for q in range(count):
                at = (OFF3 + row + q) * s3 + slot
                x33[at : at + SIDE, :] = tiles[q]
        else:
            bufs[a][off[a] + row : off[a] + row + count, slot : slot + SIDE, :] = tiles

    def receive(a):
        h, (rows, cols, c) = ROWS[a], shapes[a]
        for k in range(8):
            d = DIRS[k]
            first, count = {0: (0, rows), -1: (rows, h), 1: (-h, h)}[d[0]]
            side = 0 if d[1] < 0 else 1
            slot = cols if side == 0 else cols + SIDE

            @pl.when(reachable(axes, counts, d, -1))
            def _():
                for m in messages(a, k):
                    m.wait_recv()
                if d[1]:
                    tiles = side_in[a][side] if d[0] == 0 else corner_in[a][k - 4]
                    spread = unpacked(tiles.astype(F32), WIDTHS[a], side)
                    spread = spread[:count] if d[0] <= 0 else spread[spread.shape[0] - count :]
                    put(a, first - side, slot, spread)

            if a != 4:
                @pl.when(jnp.logical_not(reachable(axes, counts, d, -1)))
                def _():
                    if d[1]:
                        put(a, first - side, slot, jnp.zeros((count, SIDE, c), F32))
                    elif a == 0:
                        for q in range(count):
                            x33[(OFF3 + first + q) * s3 : (OFF3 + first + q) * s3 + wd3, :] = jnp.zeros((wd3, c), BF16)
                    else:
                        bufs[a][off[a] + first : off[a] + first + count, 0:cols, :] = jnp.zeros((count, cols, c), BF16)

    def pack(a, side):
        rows, cols, c = shapes[a]
        at = 0 if side == 0 else cols - SIDE
        if a == 0:
            tiles = jnp.stack([x33[(OFF3 + q) * s3 + at : (OFF3 + q) * s3 + at + SIDE, :] for q in range(rows)])
        else:
            tiles = bufs[a][off[a] : off[a] + rows, at : at + SIDE, :]
        sides[a][side] = packed(tiles.astype(F32), WIDTHS[a], side).astype(BF16)

    weight3 = 2.0 * lin3[...]
    weight2 = 2.0 * lin2[...]
    def send_all(a):
        send(a, (0, 1))
        own(a).wait()
        pack(a, 0)
        pack(a, 1)
        send(a, range(2, 8))

    def seed_rows(i):
        for q in range(2):
            p = p33[2 * i + q].astype(F32)
            t = t33[2 * i + q].astype(F32)
            seed = jnp.where(p > 0, injected(p, t, weight3), 0.0).astype(BF16)
            x33[pl.ds(pl.multiple_of((OFF3 + 2 * i + q) * s3, 16), wd3), :] = seed

    send_all(1)
    others[0].wait()
    others[1].wait()
    outer = ROWS[0] // 2

    @pl.loop(0, outer)
    def _(i):
        seed_rows(i)
        seed_rows(h3 // 2 - outer + i)

    send(0, (0, 1))

    @pl.loop(outer, h3 // 2 - outer)
    def _(i):
        seed_rows(i)

    pack(0, 0)
    pack(0, 1)
    send(0, range(2, 8))
    send_all(2)

    def masked_conv(x, w, p, y, first, rows, steps, stride, channels):
        @pl.loop(0, steps)
        def _(i):
            at = first + i * rows
            o = conv_rows(x, w, at, rows, stride, channels)
            pre = p[pl.ds(at, rows)].reshape(rows * stride, channels).astype(F32)
            y[pl.ds(pl.multiple_of(at * stride, 16), rows * stride), :] = jnp.where(pre > 0, o, 0.0).astype(BF16)

    others[2].wait()
    for j in range(wd3):
        pedge[0, j : j + 1, :] = p2[0:1, j * 128 : (j + 1) * 128]
        pedge[1, j : j + 1, :] = p2[h3 - 1 : h3, j * 128 : (j + 1) * 128]
    for a in (3, 4):
        own(a).wait()

    for j in range(wd3):
        for i0 in range(0, h3, 8):
            blk = p2[i0 : i0 + 8, j * 128 : (j + 1) * 128]
            for b in range(2):
                upp[pl.ds((OFFU + i0) * s2 + 2 * j + b, 8, stride=s2), :] = blk
    others[4].wait()
    for tap in range(9):
        dy, dx = tap // 3, tap % 3
        rows = k21v[tap * 64 : (tap + 1) * 64, :].astype(F32)
        w21[dy * c2 : (dy + 1) * c2, dx * 128 : (dx + 1) * 128] = jnp.concatenate([rows, rows], axis=0).T.astype(BF16)
    rows2 = bufs[3].shape[0]

    def inject_at(row, count, slot, width):
        p = bufs[3][pl.ds(row, count), slot : slot + width, :].reshape(count * width, c2).astype(F32)
        t = bufs[4][pl.ds(row, count), slot : slot + width, :].reshape(count * width, c2).astype(F32)
        value = injected(p, t, weight2)
        for q in range(count):
            injs[pl.ds(pl.multiple_of((row + q) * s2 + slot, 16), width), :] = value[q * width : (q + 1) * width]

    @pl.loop(0, h2 // 4)
    def _(i):
        inject_at(OFF2 + 4 * i, 4, 0, wd2)

    others[3].wait()

    @pl.loop(0, wd2 // 2)
    def _(g):
        blk = p1[:, pl.ds(pl.multiple_of(g * 128, 128), 128)]
        for a in range(2):
            twice[pl.ds(g * 2 * h2 + a, h2, stride=2), :] = blk

    send(n, range(8))
    for a in (3, 4, 5):
        send(a, (0, 1))
        if a == 5:
            own(a).wait()
        pack(a, 0)
        pack(a, 1)
        send(a, range(2, 8))
    receive(0)
    for c in weights(0):
        c.wait()
    receive(1)
    masked_conv(x33, w33, bufs[1], x32, OFF3 - 4, (h3 + 8) // 3, 3, s3, c3)
    receive(2)
    for c in weights(1):
        c.wait()
    masked_conv(x32, w32, bufs[2], x31, OFF3 - 3, (h3 + 5) // 3, 3, s3, c3)

    for k in range(8):
        @pl.when(reachable(axes, counts, DIRS[k], -1))
        def _():
            for m in messages(n, k):
                m.wait_recv()
    for b in range(2):
        upp[pl.ds((OFFU + h3) * s2 + b, wd3, stride=2), :] = prow[0]
        upp[pl.ds((OFFU - 1) * s2 + b, wd3, stride=2), :] = prow[1]
        for i0 in range(0, h3, 8):
            upp[pl.ds((OFFU + i0) * s2 + wd2 + b, 8, stride=s2), :] = pcol[0, i0 : i0 + 8]
            upp[pl.ds((OFFU + i0) * s2 + s2 - 2 + b, 8, stride=s2), :] = pcol[1, i0 : i0 + 8]
        upp[(OFFU + h3) * s2 + wd2 + b : (OFFU + h3) * s2 + wd2 + b + 1, :] = pcor[0, 0:1]
        upp[(OFFU + h3) * s2 + s2 - 2 + b : (OFFU + h3) * s2 + s2 - 2 + b + 1, :] = pcor[1, 0:1]
        upp[(OFFU - 1) * s2 + wd2 + b : (OFFU - 1) * s2 + wd2 + b + 1, :] = pcor[2, 7:8]
        upp[(OFFU - 1) * s2 + s2 - 2 + b : (OFFU - 1) * s2 + s2 - 2 + b + 1, :] = pcor[3, 7:8]

    for c in weights(2):
        c.wait()
    rows31 = (h3 + 4) // 4

    @pl.loop(0, 4)
    def _(i):
        o = conv_rows(x31, w31, OFF3 - 2 + i * rows31, rows31, s3, c2)
        for q in range(rows31):
            row = i * rows31 + q
            base = row * s2
            y = o[q * s3 : (q + 1) * s3]
            for b in range(2):
                upy[pl.ds(base + b, wd3, stride=2), :] = y[:wd3]
                upy[pl.ds(base + wd2 + b, 4, stride=2), :] = y[wd3 : wd3 + 4]
                upy[pl.ds(base + s2 + s2 - 8 + b, 4, stride=2), :] = y[s3 - 4 :]

    receive(3)
    receive(4)
    for q in range(0, rows2, SIDE):
        inject_at(q, SIDE, wd2, 2 * SIDE)
    inject_at(OFF2 - 2, 2, 0, wd2)
    inject_at(OFF2 + h2, 2, 0, wd2)
    main = s2 - 8
    par = lax.broadcasted_iota(jnp.int32, (s2, 128), 0) % 2

    @pl.loop(0, (h2 + 6) // 2)
    def _(half):
        for i in (2 * half, 2 * half + 1):
            for_row = i + OFF2 - 3
            r0 = (i + 1) // 2 + OFFU - 2
            a0 = (i + 1) % 2
            r1 = (i + 2) // 2 + OFFU - 2
            a1 = (i + 2) % 2
            at0 = pl.multiple_of(r0 * s2, 8)
            at1 = pl.multiple_of(r1 * s2 + main, 8)
            here = pl.ds(pl.multiple_of(for_row * s2, 16), s2)
            y = jnp.concatenate([upy[pl.ds(at0, main), :], upy[pl.ds(at1, 8), :]], axis=0)
            m = jnp.concatenate([upp[pl.ds(at0, main), :] - 2 * a0, upp[pl.ds(at1, 8), :] - 2 * a1], axis=0)
            p = bufs[3][for_row].astype(F32)
            arriving = jnp.where(m == par, y, 0.0) + injs[here, :]
            x22[here, :] = jnp.where(p > 0, arriving, 0.0).astype(BF16)

    receive(5)
    for c in weights(3):
        c.wait()
    masked_conv(x22, w22, bufs[5], x21, OFF2 - 2, (h2 + 3) // 5, 5, s2, c2)

    rows21 = 8

    @pl.loop(0, h2 // rows21)
    def _(i):
        o = conv_rows(x21, w21, OFF2 + i * rows21, rows21, s2, 128)
        for q in range(rows21):
            for j0 in range(0, wd2, 8):
                y = o[q * s2 + j0 : q * s2 + j0 + 8]
                for a in range(2):
                    yt[pl.ds(j0 * 2 * h2 + 2 * (i * rows21 + q) + a, 8, stride=2 * h2), :] = y

    lane_low = lax.broadcasted_iota(jnp.int32, (2 * h2, 128), 1) < 64
    want = (lax.broadcasted_iota(jnp.int32, (2 * h2, 128), 0) % 2) * 2 + jnp.where(lane_low, 0, 1)
    share = wd2 // 8
    parts = []
    for part in range(4):
        @pl.loop(0, share)
        def _(v):
            g = part * share + v
            m = twice[pl.ds(pl.multiple_of(g * 2 * h2, 8), 2 * h2), :]
            turned = pltpu.roll(m, 64, 1)
            for e in range(2):
                y = yt[pl.ds(pl.multiple_of((2 * g + e) * 2 * h2, 8), 2 * h2), :]
                sel = jnp.where(lane_low, m, turned) if e == 0 else jnp.where(lane_low, turned, m)
                res[:, pl.ds(pl.multiple_of((2 * g + e) * 128, 128), 128)] = jnp.where(sel == want, y, 0.0).astype(BF16)

        lanes = slice(part * share * 256, (part + 1) * share * 256)
        parts.append(pltpu.make_async_copy(res.at[:, lanes], out.at[:, lanes], out_sem.at[part]))
        parts[-1].start()
    for a in range(n + 1):
        for k in range(8):
            @pl.when(reachable(axes, counts, DIRS[k], 1))
            def _():
                for m in messages(a, k):
                    m.wait_send()
    for c in parts:
        c.wait()


def shards(axes, counts, relu21, relu22, relu31, relu32, relu33, target22, target33, pool1, pool2, lin2, lin3,
           k21, k22, k31, k32, k33):
    tensors = (relu33, target33, relu32, relu31, relu22, target22, relu21)
    shapes = tuple(t.shape for t in (relu33, relu32, relu31, relu22, target22, relu21))
    h3, wd3, c3 = relu33.shape
    h2, wd2, c2 = relu22.shape
    s3, s2 = wd3 + 2 * SIDE, wd2 + 2 * SIDE
    anywhere = pl.BlockSpec(memory_space=pl.ANY)
    vmem = pl.BlockSpec(memory_space=pltpu.VMEM)
    rows3, rows2 = h3 + 2 * OFF3, h2 + 2 * OFF2
    per = [SIDE // w for w in WIDTHS]
    scratch = [pltpu.VMEM((h3, wd3, c3), BF16)] * 2
    scratch += [pltpu.VMEM((rows3, s3, c3), BF16)] * 2 + [pltpu.VMEM((rows2, s2, c2), BF16)] * 3
    scratch += [pltpu.VMEM((2, s[0] // k, SIDE, s[2]), BF16) for s, k in zip(shapes, per)] * 2
    scratch += [pltpu.VMEM((4, -(-r // k), SIDE, s[2]), BF16) for s, k, r in zip(shapes, per, ROWS)]
    scratch += [pltpu.VMEM((rows3 * s3, c3), BF16)] * 3 + [pltpu.VMEM((rows2 * s2, c2), BF16)] * 2
    scratch += [pltpu.VMEM((3 * k.shape[0], k.shape[1] // 3), BF16) for k in (k33, k32, k31, k22)]
    scratch += [
        pltpu.VMEM((3 * c2, 384), BF16),
        pltpu.VMEM(k21.shape[::-1], BF16),
        pltpu.VMEM(pool1.shape, jnp.int32),
        pltpu.VMEM(pool2.shape, jnp.int32),
        pltpu.VMEM((2, wd3, 128), jnp.int32),
        pltpu.VMEM((2, wd3, 128), jnp.int32),
        pltpu.VMEM((2, h3, 128), jnp.int32),
        pltpu.VMEM((4, 8, 128), jnp.int32),
        pltpu.VMEM(((h3 + 2 * OFFU + 1) * s2, 128), F32),
        pltpu.VMEM(((h3 + 2 * OFFU + 1) * s2, 128), jnp.int32),
        pltpu.VMEM((wd2 * 2 * h2, 128), F32),
        pltpu.VMEM((wd2 * h2, 128), jnp.int32),
        pltpu.VMEM((rows2 * s2, c2), F32),
        pltpu.VMEM((2 * h2, wd2 * 128), BF16),
        pltpu.SemaphoreType.DMA((6,)),
        pltpu.SemaphoreType.DMA((4, 3)),
        pltpu.SemaphoreType.DMA((5,)),
        pltpu.SemaphoreType.DMA((2, 4)),
        pltpu.SemaphoreType.DMA((2, 4)),
        pltpu.SemaphoreType.DMA((7, 8)),
        pltpu.SemaphoreType.DMA((7, 8)),
        pltpu.SemaphoreType.DMA((4,)),
    ]
    return pl.pallas_call(
        functools.partial(body_kernel, axes, counts, shapes),
        out_shape=jax.ShapeDtypeStruct((2 * h2, wd2 * 128), BF16),
        in_specs=[anywhere] * 9 + [vmem] * 2 + [anywhere] * 5,
        out_specs=anywhere,
        scratch_shapes=scratch,
        compiler_params=pltpu.CompilerParams(
            vmem_limit_bytes=56 * 1024 * 1024, collective_id=0, has_side_effects=True),
        name="body",
    )(*tensors, pool1, pool2, lin2.reshape(1, c2), lin3.reshape(1, c3), k21.T, k22, k31, k32, k33)


def solution(mesh):
    axes = ("row", "col")
    counts = tuple(mesh.shape[a] for a in axes)
    cells = P("row", "col", None)
    in_specs = (cells,) * 7 + (P("row", "col"),) * 2 + (P(),) * 7
    return jax.shard_map(functools.partial(shards, axes, counts), mesh=mesh, in_specs=in_specs,
                         out_specs=P("row", "col"), check_vma=False)
```

```python
import functools

import jax
import jax.numpy as jnp
from jax import lax
from jax.experimental import pallas as pl
from jax.experimental.pallas import tpu as pltpu
from jax.sharding import PartitionSpec as P

EPSILON = 1e-06
MESH = pl.DeviceIdType.MESH
F32 = jnp.float32
BF16 = jnp.bfloat16
SIDE = 8
OFF3 = 6
OFF2 = 4
OFFU = 2
DIRS = ((-1, 0), (1, 0), (0, -1), (0, 1), (-1, -1), (-1, 1), (1, -1), (1, 1))


WIDTHS = (4, 4, 2, 2, 2, 1)
ROWS = (4, 3, 2, 2, 2, 1)


def reachable(axes, counts, d, sign):
    checks = []
    for axis, count, step in zip(axes, counts, d):
        if step:
            target = lax.axis_index(axis) + sign * step
            checks.append(target >= 0 if sign * step < 0 else target < count)
    ok = checks[0]
    for c in checks[1:]:
        ok = jnp.logical_and(ok, c)
    return ok


def packed(tiles, width, side):
    k = SIDE // width
    rows, _, c = tiles.shape
    grouped = tiles.reshape(rows // k, k, SIDE, c)
    sub = lax.broadcasted_iota(jnp.int32, (rows // k, SIDE, c), 1)
    total = None
    for i in range(k):
        shift = (i * width - (0 if side == 0 else SIDE - width)) % SIDE
        piece = grouped[:, i]
        if shift:
            piece = pltpu.roll(piece, shift, 1)
        total = piece if total is None else jnp.where(sub >= i * width, piece, total)
    return total


def unpacked(tiles, width, side):
    k = SIDE // width
    count, _, c = tiles.shape
    pieces = []
    for i in range(k):
        shift = ((0 if side == 0 else SIDE - width) - i * width) % SIDE
        pieces.append(pltpu.roll(tiles, shift, 1) if shift else tiles)
    return jnp.stack(pieces, axis=1).reshape(count * k, SIDE, c)


def injected(p, t, weight):
    f = jnp.maximum(p, 0.0)
    g = jnp.maximum(t, 0.0)
    rinv = lax.rsqrt(jnp.mean(f * f, axis=-1, keepdims=True) + EPSILON)
    sinv = lax.rsqrt(jnp.mean(g * g, axis=-1, keepdims=True) + EPSILON)
    u = f * rinv
    e = weight * (u - g * sinv)
    return (e - u * jnp.mean(e * u, axis=-1, keepdims=True)) * rinv


def shifted_sum(z, n):
    length = z.shape[0]
    return pltpu.roll(z[:, :n], length - 1, 0) + z[:, n : 2 * n] + pltpu.roll(z[:, 2 * n :], 1, 0)


def conv_rows(x, w, first, rows, stride, n):
    length = rows * stride + 32
    start = first * stride - 16
    parts = [x[pl.ds(pl.multiple_of(start + (1 - dy) * stride, 16), length), :] for dy in range(3)]
    z = jnp.dot(jnp.concatenate(parts, axis=1), w[...], preferred_element_type=F32)
    return shifted_sum(z, n)[16 : 16 + rows * stride]


def body_kernel(axes, counts, shapes, *refs):
    (relu33, target33, relu32, relu31, relu22, target22, relu21,
     pool1, pool2, lin2, lin3, k21, k22, k31, k32, k33, out) = refs[:17]
    scratch = refs[17:]
    inputs = (None, relu32, relu31, relu22, target22, relu21)
    p33, t33 = scratch[:2]
    bufs = (None,) + tuple(scratch[2:7])
    sides, side_in, corner_in = scratch[7:13], scratch[13:19], scratch[19:25]
    (x33, x32, x31, x22, x21, w33, w32, w31, w22, w21, k21v, p1, p2, pedge, prow, pcol, pcor, upy, upp, yt, twice, injs, res,
     own_sem, w_sem, misc_sem, seed_send, seed_recv, send_sem, recv_sem, out_sem) = scratch[25:]
    n = 6
    off = [OFF3, OFF3, OFF3, OFF2, OFF2, OFF2]
    h3, wd3, c3 = shapes[0]
    h2, wd2, c2 = shapes[3]
    s3, s2 = wd3 + 2 * SIDE, wd2 + 2 * SIDE

    def own(a):
        return pltpu.make_async_copy(
            inputs[a], bufs[a].at[off[a] : off[a] + shapes[a][0], 0 : shapes[a][1]], own_sem.at[a])

    def weights(i):
        k, w = ((k33, w33), (k32, w32), (k31, w31), (k22, w22))[i]
        o, cols = k.shape[0], k.shape[1] // 3
        return [pltpu.make_async_copy(k.at[:, dy * cols : (dy + 1) * cols], w.at[dy * o : (dy + 1) * o], w_sem.at[i, dy])
                for dy in range(3)]

    others = [pltpu.make_async_copy(src, dst, misc_sem.at[i])
              for i, (src, dst) in enumerate(((relu33, p33), (target33, t33), (pool2, p2), (pool1, p1), (k21, k21v)))]
    others[0].start()
    others[1].start()
    for a in (1, 2, 3, 4, 5):
        own(a).start()
    others[2].start()
    for i in range(4):
        for c in weights(i):
            c.start()
    others[4].start()
    others[3].start()

    me = tuple(lax.axis_index(axis) for axis in axes)

    def peer(d):
        return (me[0] + d[0], me[1] + d[1])

    barrier = pltpu.get_barrier_semaphore()
    for d in DIRS:
        @pl.when(reachable(axes, counts, d, 1))
        def _():
            pl.semaphore_signal(barrier, inc=1, device_id=peer(d), device_id_type=MESH)
    spans = [1 + jnp.minimum(m, 1) + jnp.minimum(c - 1 - m, 1) for m, c in zip(me, counts)]
    pl.semaphore_wait(barrier, spans[0] * spans[1] - 1)

    def remote(src, dst, ssem, rsem, d):
        return pltpu.make_async_remote_copy(
            src_ref=src, dst_ref=dst, send_sem=ssem, recv_sem=rsem, device_id=peer(d), device_id_type=MESH)

    def corner_tiles(a):
        k = SIDE // WIDTHS[a]
        return -(-ROWS[a] // k)

    def messages(a, k):
        d = DIRS[k]
        ssem, rsem = send_sem.at[a, k], recv_sem.at[a, k]
        if a == n:
            if d[1] == 0:
                return [remote(pedge.at[k], prow.at[k], ssem, rsem, d)]
            rows = {0: slice(0, h3), -1: slice(0, 8), 1: slice(h3 - 8, h3)}[d[0]]
            lanes = slice(0, 128) if d[1] < 0 else slice((wd3 - 1) * 128, wd3 * 128)
            dst = pcol.at[k - 2] if d[0] == 0 else pcor.at[k - 4]
            return [remote(pool2.at[rows, lanes], dst, ssem, rsem, d)]
        if d[1] == 0:
            h, rows = ROWS[a], shapes[a][0]
            first, land = (0, rows) if d[0] < 0 else (rows - h, -h)
            if a == 0:
                return [remote(x33.at[(OFF3 + first + q) * s3 : (OFF3 + first + q) * s3 + wd3],
                               x33.at[(OFF3 + land + q) * s3 : (OFF3 + land + q) * s3 + wd3],
                               seed_send.at[k, q], seed_recv.at[k, q], d) for q in range(h)]
            return [remote(inputs[a].at[first : first + h],
                           bufs[a].at[off[a] + land : off[a] + land + h, 0 : shapes[a][1]], ssem, rsem, d)]
        side = 0 if d[1] < 0 else 1
        if d[0] == 0:
            return [remote(sides[a].at[side], side_in[a].at[side], ssem, rsem, d)]
        tiles, total = corner_tiles(a), sides[a].shape[1]
        first = 0 if d[0] < 0 else total - tiles
        return [remote(sides[a].at[side, first : first + tiles], corner_in[a].at[k - 4], ssem, rsem, d)]

    def send(a, ks):
        for k in ks:
            @pl.when(reachable(axes, counts, DIRS[k], 1))
            def _():
                for c in messages(a, k):
                    c.start()

    def put(a, row, slot, tiles):
        count = tiles.shape[0]
        tiles = tiles.astype(BF16)
        if a == 0:
            for q in range(count):
                at = (OFF3 + row + q) * s3 + slot
                x33[at : at + SIDE, :] = tiles[q]
        else:
            bufs[a][off[a] + row : off[a] + row + count, slot : slot + SIDE, :] = tiles

    def receive(a):
        h, (rows, cols, c) = ROWS[a], shapes[a]
        for k in range(8):
            d = DIRS[k]
            first, count = {0: (0, rows), -1: (rows, h), 1: (-h, h)}[d[0]]
            side = 0 if d[1] < 0 else 1
            slot = cols if side == 0 else cols + SIDE

            @pl.when(reachable(axes, counts, d, -1))
            def _():
                for m in messages(a, k):
                    m.wait_recv()
                if d[1]:
                    tiles = side_in[a][side] if d[0] == 0 else corner_in[a][k - 4]
                    spread = unpacked(tiles.astype(F32), WIDTHS[a], side)
                    spread = spread[:count] if d[0] <= 0 else spread[spread.shape[0] - count :]
                    put(a, first - side, slot, spread)

            if a != 4:
                @pl.when(jnp.logical_not(reachable(axes, counts, d, -1)))
                def _():
                    if d[1]:
                        put(a, first - side, slot, jnp.zeros((count, SIDE, c), F32))
                    elif a == 0:
                        for q in range(count):
                            x33[(OFF3 + first + q) * s3 : (OFF3 + first + q) * s3 + wd3, :] = jnp.zeros((wd3, c), BF16)
                    else:
                        bufs[a][off[a] + first : off[a] + first + count, 0:cols, :] = jnp.zeros((count, cols, c), BF16)

    def pack(a, side):
        rows, cols, c = shapes[a]
        at = 0 if side == 0 else cols - SIDE
        if a == 0:
            tiles = jnp.stack([x33[(OFF3 + q) * s3 + at : (OFF3 + q) * s3 + at + SIDE, :] for q in range(rows)])
        else:
            tiles = bufs[a][off[a] : off[a] + rows, at : at + SIDE, :]
        sides[a][side] = packed(tiles.astype(F32), WIDTHS[a], side).astype(BF16)

    weight3 = 2.0 * lin3[...]
    weight2 = 2.0 * lin2[...]
    def send_all(a):
        send(a, (0, 1))
        own(a).wait()
        pack(a, 0)
        pack(a, 1)
        send(a, range(2, 8))

    def seed_rows(i):
        for q in range(2):
            p = p33[2 * i + q].astype(F32)
            t = t33[2 * i + q].astype(F32)
            seed = jnp.where(p > 0, injected(p, t, weight3), 0.0).astype(BF16)
            x33[pl.ds(pl.multiple_of((OFF3 + 2 * i + q) * s3, 16), wd3), :] = seed

    send_all(1)
    others[0].wait()
    others[1].wait()
    outer = ROWS[0] // 2

    @pl.loop(0, outer)
    def _(i):
        seed_rows(i)
        seed_rows(h3 // 2 - outer + i)

    send(0, (0, 1))

    @pl.loop(outer, h3 // 2 - outer)
    def _(i):
        seed_rows(i)

    pack(0, 0)
    pack(0, 1)
    send(0, range(2, 8))
    send_all(2)

    def masked_conv(x, w, p, y, first, rows, steps, stride, channels):
        @pl.loop(0, steps)
        def _(i):
            at = first + i * rows
            o = conv_rows(x, w, at, rows, stride, channels)
            pre = p[pl.ds(at, rows)].reshape(rows * stride, channels).astype(F32)
            y[pl.ds(pl.multiple_of(at * stride, 16), rows * stride), :] = jnp.where(pre > 0, o, 0.0).astype(BF16)

    others[2].wait()
    for j in range(wd3):
        pedge[0, j : j + 1, :] = p2[0:1, j * 128 : (j + 1) * 128]
        pedge[1, j : j + 1, :] = p2[h3 - 1 : h3, j * 128 : (j + 1) * 128]
    for a in (3, 4):
        own(a).wait()

    for j in range(wd3):
        for i0 in range(0, h3, 8):
            blk = p2[i0 : i0 + 8, j * 128 : (j + 1) * 128]
            for b in range(2):
                upp[pl.ds((OFFU + i0) * s2 + 2 * j + b, 8, stride=s2), :] = blk
    others[4].wait()
    for tap in range(9):
        dy, dx = tap // 3, tap % 3
        rows = k21v[tap * 64 : (tap + 1) * 64, :].astype(F32)
        w21[dy * c2 : (dy + 1) * c2, dx * 128 : (dx + 1) * 128] = jnp.concatenate([rows, rows], axis=0).T.astype(BF16)
    rows2 = bufs[3].shape[0]

    def inject_at(row, count, slot, width):
        p = bufs[3][pl.ds(row, count), slot : slot + width, :].reshape(count * width, c2).astype(F32)
        t = bufs[4][pl.ds(row, count), slot : slot + width, :].reshape(count * width, c2).astype(F32)
        value = injected(p, t, weight2)
        for q in range(count):
            injs[pl.ds(pl.multiple_of((row + q) * s2 + slot, 16), width), :] = value[q * width : (q + 1) * width]

    @pl.loop(0, h2 // 4)
    def _(i):
        inject_at(OFF2 + 4 * i, 4, 0, wd2)

    others[3].wait()

    @pl.loop(0, wd2 // 2)
    def _(g):
        blk = p1[:, pl.ds(pl.multiple_of(g * 128, 128), 128)]
        for a in range(2):
            twice[pl.ds(g * 2 * h2 + a, h2, stride=2), :] = blk

    send(n, range(8))
    for a in (3, 4, 5):
        send(a, (0, 1))
        if a == 5:
            own(a).wait()
        pack(a, 0)
        pack(a, 1)
        send(a, range(2, 8))
    receive(0)
    for c in weights(0):
        c.wait()
    receive(1)
    masked_conv(x33, w33, bufs[1], x32, OFF3 - 4, (h3 + 8) // 3, 3, s3, c3)
    receive(2)
    for c in weights(1):
        c.wait()
    masked_conv(x32, w32, bufs[2], x31, OFF3 - 3, (h3 + 5) // 3, 3, s3, c3)

    for k in range(8):
        @pl.when(reachable(axes, counts, DIRS[k], -1))
        def _():
            for m in messages(n, k):
                m.wait_recv()
    for b in range(2):
        upp[pl.ds((OFFU + h3) * s2 + b, wd3, stride=2), :] = prow[0]
        upp[pl.ds((OFFU - 1) * s2 + b, wd3, stride=2), :] = prow[1]
        for i0 in range(0, h3, 8):
            upp[pl.ds((OFFU + i0) * s2 + wd2 + b, 8, stride=s2), :] = pcol[0, i0 : i0 + 8]
            upp[pl.ds((OFFU + i0) * s2 + s2 - 2 + b, 8, stride=s2), :] = pcol[1, i0 : i0 + 8]
        upp[(OFFU + h3) * s2 + wd2 + b : (OFFU + h3) * s2 + wd2 + b + 1, :] = pcor[0, 0:1]
        upp[(OFFU + h3) * s2 + s2 - 2 + b : (OFFU + h3) * s2 + s2 - 2 + b + 1, :] = pcor[1, 0:1]
        upp[(OFFU - 1) * s2 + wd2 + b : (OFFU - 1) * s2 + wd2 + b + 1, :] = pcor[2, 7:8]
        upp[(OFFU - 1) * s2 + s2 - 2 + b : (OFFU - 1) * s2 + s2 - 2 + b + 1, :] = pcor[3, 7:8]

    for c in weights(2):
        c.wait()
    rows31 = (h3 + 4) // 4

    @pl.loop(0, 4)
    def _(i):
        o = conv_rows(x31, w31, OFF3 - 2 + i * rows31, rows31, s3, c2)
        for q in range(rows31):
            row = i * rows31 + q
            base = row * s2
            y = o[q * s3 : (q + 1) * s3]
            for b in range(2):
                upy[pl.ds(base + b, wd3, stride=2), :] = y[:wd3]
                upy[pl.ds(base + wd2 + b, 4, stride=2), :] = y[wd3 : wd3 + 4]
                upy[pl.ds(base + s2 + s2 - 8 + b, 4, stride=2), :] = y[s3 - 4 :]

    receive(3)
    receive(4)
    for q in range(0, rows2, SIDE):
        inject_at(q, SIDE, wd2, 2 * SIDE)
    inject_at(OFF2 - 2, 2, 0, wd2)
    inject_at(OFF2 + h2, 2, 0, wd2)
    main = s2 - 8
    par = lax.broadcasted_iota(jnp.int32, (s2, 128), 0) % 2

    @pl.loop(0, (h2 + 6) // 2)
    def _(half):
        for i in (2 * half, 2 * half + 1):
            for_row = i + OFF2 - 3
            r0 = (i + 1) // 2 + OFFU - 2
            a0 = (i + 1) % 2
            r1 = (i + 2) // 2 + OFFU - 2
            a1 = (i + 2) % 2
            at0 = pl.multiple_of(r0 * s2, 8)
            at1 = pl.multiple_of(r1 * s2 + main, 8)
            here = pl.ds(pl.multiple_of(for_row * s2, 16), s2)
            y = jnp.concatenate([upy[pl.ds(at0, main), :], upy[pl.ds(at1, 8), :]], axis=0)
            m = jnp.concatenate([upp[pl.ds(at0, main), :] - 2 * a0, upp[pl.ds(at1, 8), :] - 2 * a1], axis=0)
            p = bufs[3][for_row].astype(F32)
            arriving = jnp.where(m == par, y, 0.0) + injs[here, :]
            x22[here, :] = jnp.where(p > 0, arriving, 0.0).astype(BF16)

    receive(5)
    for c in weights(3):
        c.wait()
    masked_conv(x22, w22, bufs[5], x21, OFF2 - 2, (h2 + 3) // 5, 5, s2, c2)

    rows21 = 8

    @pl.loop(0, h2 // rows21)
    def _(i):
        o = conv_rows(x21, w21, OFF2 + i * rows21, rows21, s2, 128)
        for q in range(rows21):
            for j0 in range(0, wd2, 8):
                y = o[q * s2 + j0 : q * s2 + j0 + 8]
                for a in range(2):
                    yt[pl.ds(j0 * 2 * h2 + 2 * (i * rows21 + q) + a, 8, stride=2 * h2), :] = y

    lane_low = lax.broadcasted_iota(jnp.int32, (2 * h2, 128), 1) < 64
    want = (lax.broadcasted_iota(jnp.int32, (2 * h2, 128), 0) % 2) * 2 + jnp.where(lane_low, 0, 1)
    share = wd2 // 8
    parts = []
    for part in range(4):
        @pl.loop(0, share // 2)
        def _(v):
            for u in range(2):
                g = part * share + 2 * v + u
                m = twice[pl.ds(pl.multiple_of(g * 2 * h2, 8), 2 * h2), :]
                turned = pltpu.roll(m, 64, 1)
                for e in range(2):
                    y = yt[pl.ds(pl.multiple_of((2 * g + e) * 2 * h2, 8), 2 * h2), :]
                    sel = jnp.where(lane_low, m, turned) if e == 0 else jnp.where(lane_low, turned, m)
                    to = pl.ds(pl.multiple_of((2 * g + e) * 128, 128), 128)
                    res[:, to] = jnp.where(sel == want, y, 0.0).astype(BF16)

        lanes = slice(part * share * 256, (part + 1) * share * 256)
        parts.append(pltpu.make_async_copy(res.at[:, lanes], out.at[:, lanes], out_sem.at[part]))
        parts[-1].start()
    for a in range(n + 1):
        for k in range(8):
            @pl.when(reachable(axes, counts, DIRS[k], 1))
            def _():
                for m in messages(a, k):
                    m.wait_send()
    for c in parts:
        c.wait()


def shards(axes, counts, relu21, relu22, relu31, relu32, relu33, target22, target33, pool1, pool2, lin2, lin3,
           k21, k22, k31, k32, k33):
    tensors = (relu33, target33, relu32, relu31, relu22, target22, relu21)
    shapes = tuple(t.shape for t in (relu33, relu32, relu31, relu22, target22, relu21))
    h3, wd3, c3 = relu33.shape
    h2, wd2, c2 = relu22.shape
    s3, s2 = wd3 + 2 * SIDE, wd2 + 2 * SIDE
    anywhere = pl.BlockSpec(memory_space=pl.ANY)
    vmem = pl.BlockSpec(memory_space=pltpu.VMEM)
    rows3, rows2 = h3 + 2 * OFF3, h2 + 2 * OFF2
    per = [SIDE // w for w in WIDTHS]
    scratch = [pltpu.VMEM((h3, wd3, c3), BF16)] * 2
    scratch += [pltpu.VMEM((rows3, s3, c3), BF16)] * 2 + [pltpu.VMEM((rows2, s2, c2), BF16)] * 3
    scratch += [pltpu.VMEM((2, s[0] // k, SIDE, s[2]), BF16) for s, k in zip(shapes, per)] * 2
    scratch += [pltpu.VMEM((4, -(-r // k), SIDE, s[2]), BF16) for s, k, r in zip(shapes, per, ROWS)]
    scratch += [pltpu.VMEM((rows3 * s3, c3), BF16)] * 3 + [pltpu.VMEM((rows2 * s2, c2), BF16)] * 2
    scratch += [pltpu.VMEM((3 * k.shape[0], k.shape[1] // 3), BF16) for k in (k33, k32, k31, k22)]
    scratch += [
        pltpu.VMEM((3 * c2, 384), BF16),
        pltpu.VMEM(k21.shape[::-1], BF16),
        pltpu.VMEM(pool1.shape, jnp.int32),
        pltpu.VMEM(pool2.shape, jnp.int32),
        pltpu.VMEM((2, wd3, 128), jnp.int32),
        pltpu.VMEM((2, wd3, 128), jnp.int32),
        pltpu.VMEM((2, h3, 128), jnp.int32),
        pltpu.VMEM((4, 8, 128), jnp.int32),
        pltpu.VMEM(((h3 + 2 * OFFU + 1) * s2, 128), F32),
        pltpu.VMEM(((h3 + 2 * OFFU + 1) * s2, 128), jnp.int32),
        pltpu.VMEM((wd2 * 2 * h2, 128), F32),
        pltpu.VMEM((wd2 * h2, 128), jnp.int32),
        pltpu.VMEM((rows2 * s2, c2), F32),
        pltpu.VMEM((2 * h2, wd2 * 128), BF16),
        pltpu.SemaphoreType.DMA((6,)),
        pltpu.SemaphoreType.DMA((4, 3)),
        pltpu.SemaphoreType.DMA((5,)),
        pltpu.SemaphoreType.DMA((2, 4)),
        pltpu.SemaphoreType.DMA((2, 4)),
        pltpu.SemaphoreType.DMA((7, 8)),
        pltpu.SemaphoreType.DMA((7, 8)),
        pltpu.SemaphoreType.DMA((4,)),
    ]
    return pl.pallas_call(
        functools.partial(body_kernel, axes, counts, shapes),
        out_shape=jax.ShapeDtypeStruct((2 * h2, wd2 * 128), BF16),
        in_specs=[anywhere] * 9 + [vmem] * 2 + [anywhere] * 5,
        out_specs=anywhere,
        scratch_shapes=scratch,
        compiler_params=pltpu.CompilerParams(
            vmem_limit_bytes=56 * 1024 * 1024, collective_id=0, has_side_effects=True),
        name="body",
    )(*tensors, pool1, pool2, lin2.reshape(1, c2), lin3.reshape(1, c3), k21.T, k22, k31, k32, k33)


def solution(mesh):
    axes = ("row", "col")
    counts = tuple(mesh.shape[a] for a in axes)
    cells = P("row", "col", None)
    in_specs = (cells,) * 7 + (P("row", "col"),) * 2 + (P(),) * 7
    return jax.shard_map(functools.partial(shards, axes, counts), mesh=mesh, in_specs=in_specs,
                         out_specs=P("row", "col"), check_vma=False)
```
